256 devices in a mesh: tm: 64 (over z, y, core), state: 4 (over x).
Axes of the slice: x: 4, y: 4, z: 8, core: 2. Of those that a mesh axis runs over, the one named last changes fastest.
Arguments:
- updated_spread: float32 [256, 512, 512], P('tm', 'state'), may hold values from -1 to 1, as said below
- inverse_prior_spread: float32 [256, 512, 512], P('tm', 'state'), may hold values from -1 to 1, as said below
- dynamics_tiles: float32 [256, 8, 64, 128], P('tm', 'state'), may hold values from -0.15625 to 0.15625
- tile_column_ids: int32 [256, 8, 2], P('tm'), may hold values from 0 to 7, all different within a row
- updated_average: float32 [256, 512], P('tm', 'state'), may hold values from -1.5 to 1.5
- prior_average: float32 [256, 512], P('tm', 'state'), may hold values from -1.5 to 1.5
Outputs:
- smoothed_mean: float32 [256, 512], P('tm', 'state')
The draws below stay inside these ranges and needn't reach their ends.
Inputs may be any that keep to these rules, and one draw needn't show every extreme that they name: `updated_spread`: each filtered covariance is exactly symmetric. `inverse_prior_spread`: each predicted precision is exactly symmetric. `tile_column_ids`: the 2 block columns listed for one block row differ.
All inputs are finite; a program needn't handle non-finite values.
Results may differ from the reference program's by a relative error of at most 0.0003.
Values sent between devices are 32-bit elements; how exact they have to be, the bound alone decides.
No kernel may reach another device: no remote copies, remote signals or barrier semaphores. Data moves between devices by JAX's collectives and lax.ppermute only.
A program may use at most 192 MiB of HBM per device.

```python
import math
import jax
import jax.numpy as jnp
from jax import lax

STATE = 512
BS = 64
NNZ = 2
NB = 8
TIME_STEP_TOTAL = 256


def draw_updated_spread(key, part):
    random_keys_list = jax.random.split(key, 4)
    rates = jnp.exp(jax.random.uniform(random_keys_list[0], (STATE,), jnp.float32, math.log(1.0 / (2 * TIME_STEP_TOTAL)), math.log(1.0 / 20)))
    noise = jnp.clip(jax.random.normal(random_keys_list[3], (TIME_STEP_TOTAL, STATE, STATE), jnp.float32), -4.0, 4.0)
    jump_location = jax.random.randint(random_keys_list[1], (3,), 0, TIME_STEP_TOTAL)
    random_jump = jnp.any(jnp.arange(TIME_STEP_TOTAL)[:, None] == jump_location[None, :], axis=1)
    multiplier_term = jax.random.uniform(random_keys_list[2], (TIME_STEP_TOTAL,), jnp.float32, 0.5, 0.8)
    noise_scale = jnp.where(random_jump, multiplier_term, 1.0)
    diagonal = jnp.exp(-rates)[None, :] * noise_scale[:, None]
    noise = noise * (0.3 / math.sqrt(STATE))
    symmetric = (noise + jnp.swapaxes(noise, 1, 2)) * 0.70710678
    identity = jnp.eye(STATE, dtype=jnp.float32)[None]
    return symmetric * (1.0 - identity) + identity * diagonal[:, :, None]


def draw_inverse_prior_spread(key, part):
    random_keys_list = jax.random.split(key, 2)
    diagonal = jax.random.uniform(random_keys_list[0], (TIME_STEP_TOTAL, STATE), jnp.float32, 0.88, 0.98)
    noise = jnp.clip(jax.random.normal(random_keys_list[1], (TIME_STEP_TOTAL, STATE, STATE), jnp.float32), -4.0, 4.0)
    noise = noise * (0.2 / math.sqrt(STATE))
    symmetric = (noise + jnp.swapaxes(noise, 1, 2)) * 0.70710678
    identity = jnp.eye(STATE, dtype=jnp.float32)[None]
    return symmetric * (1.0 - identity) + identity * diagonal[:, :, None]


def level_of(key, extent, pieces, least, high):
    loudness = 1.0
    for dim, parts in pieces:
        heights = jax.random.uniform(jax.random.fold_in(jax.random.fold_in(key, 6), dim), (parts,), jnp.float32, least / len(pieces), high / len(pieces))
        loudness = loudness * jnp.repeat(jnp.exp(heights), extent[dim] // parts).reshape((-1,) + (1,) * (len(extent) - 1 - dim))
    return loudness


def choose_distinct(rng, rows, count, top, lift):
    sequence = jax.random.permutation(jax.random.fold_in(rng, 1), count)
    boost = sequence
    for power in range(3):
        boost = boost * boost // count
    boost = boost * lift // count
    tickets = jax.random.randint(jax.random.fold_in(rng, 2), (rows, count), 0, 4096) + boost
    sure = jax.random.permutation(jax.random.fold_in(rng, 3), rows)[jnp.arange(count) % rows]
    tickets = jnp.where(jnp.arange(rows)[:, None] == sure[None, :], 1 << 14, tickets)
    merit = tickets * count + jnp.arange(count)
    return lax.top_k(merit.astype(jnp.int32), top)[1].astype(jnp.int32)


def scatter_about(stream_key, extent, deviation, most, cuts=(), kind=jnp.bfloat16):
    drawn = deviation * jax.random.normal(stream_key, extent, jnp.float32)
    if cuts:
        drawn = drawn * level_of(stream_key, extent, cuts, -0.22, 0.18)
    return jnp.clip(drawn, -most, most).astype(kind)


def setup_inputs(seed: int = 0) -> dict:
    key_of = jax.random.split(jax.random.key(seed), 7)
    updated_spread = draw_updated_spread(jax.random.fold_in(key_of[6], 71), 0)
    inverse_prior_spread = draw_inverse_prior_spread(jax.random.fold_in(key_of[6], 71), 0)
    dynamics_tiles = scatter_about(key_of[2], (TIME_STEP_TOTAL, NB, BS, NNZ * BS), (11 * NNZ * BS) ** -0.5, 0.15625, ((0, 64), (1, 4)), jnp.float32)
    tile_column_ids = choose_distinct(key_of[3], TIME_STEP_TOTAL * NB, NB, NNZ, 0).reshape((TIME_STEP_TOTAL, NB, NNZ))
    updated_average = scatter_about(key_of[4], (TIME_STEP_TOTAL, STATE), 0.25, 1.5, ((0, 64), (1, 4)), jnp.float32)
    prior_average = scatter_about(key_of[5], (TIME_STEP_TOTAL, STATE), 0.25, 1.5, ((0, 64), (1, 4)), jnp.float32)
    return dict(updated_spread=updated_spread, inverse_prior_spread=inverse_prior_spread, dynamics_tiles=dynamics_tiles, tile_column_ids=tile_column_ids, updated_average=updated_average, prior_average=prior_average)


finest_accuracy = lax.Precision.HIGHEST


def dense_increment(values, columns):
    block_count = columns.shape[0]
    pick = (columns[:, :, None] == jnp.arange(block_count, dtype=jnp.int32)[None, None, :]).astype(jnp.float32)
    blocks = values.reshape(block_count, BS, NNZ, BS)
    dense = jnp.einsum('rjc,rajb->racb', pick, blocks, precision=finest_accuracy)
    return dense.reshape(block_count * BS, block_count * BS)


def reference(updated_spread, inverse_prior_spread, dynamics_tiles, tile_column_ids, updated_average, prior_average):
    def reversed_pass(carry, inputs):
        covariance, accuracy_setting, values, columns, mean_now, mean_next, position = inputs
        increment = dense_increment(values, columns)
        left_part = covariance + jnp.dot(covariance, increment.T, precision=finest_accuracy)
        gain = jnp.dot(left_part, accuracy_setting, precision=finest_accuracy)
        offset = mean_now - jnp.dot(gain, mean_next, precision=finest_accuracy)
        last_step = position == TIME_STEP_TOTAL - 1
        gain = jnp.where(last_step, jnp.zeros_like(gain), gain)
        offset = jnp.where(last_step, mean_now, offset)
        carry = jnp.dot(gain, carry, precision=finest_accuracy) + offset
        return carry, carry

    placement_ids = jnp.arange(TIME_STEP_TOTAL, dtype=jnp.int32)
    beginning_index = jnp.zeros((STATE,), jnp.float32)
    unused_item, refined_result = lax.scan(reversed_pass, beginning_index, (updated_spread, inverse_prior_spread, dynamics_tiles, tile_column_ids, updated_average, prior_average, placement_ids), reverse=True)
    return refined_result
```

```python
import jax
import jax.numpy as jnp
from jax import lax
from jax.experimental import pallas as pl
from jax.experimental.pallas import tpu as pltpu
from jax.sharding import PartitionSpec as P

NZ, NY, NC, NX = 8, 4, 2, 4
W = 512
B = 128
HALF = 256
PAN = HALF + 8
FULL = W + 8
AXES = ("tm", "state")
F32 = jnp.float32
VMEM_LIMIT = 56 * 1024 * 1024


def joint(move):
    pairs = []
    for z in range(NZ):
        for y in range(NY):
            for c in range(NC):
                for x in range(NX):
                    y2, c2, x2 = move(y, c, x)
                    source = ((z * NY + y) * NC + c) * NX + x
                    pairs.append((source, ((z * NY + y2) * NC + c2) * NX + x2))
    return pairs


def spread_move(p):
    def move(y, c, x):
        q = (x + p) % 4
        return y, q % 2, 2 * c + q // 2

    return move


def collect_move(r):
    def move(y, c, x):
        return y, x // 2, 2 * c + (x + r) % 2

    return move


SWAP = joint(lambda y, c, x: (y, 1 - c, x))
SPREAD = [joint(spread_move(p)) for p in range(4)]
COLLECT = [joint(collect_move(r)) for r in range(2)]
SHIFT_X = {k: joint(lambda y, c, x, k=k: (y, c, (x + k) % 4)) for k in (1, 2, 3)}
SHIFT_Y = {k: joint(lambda y, c, x, k=k: ((y + k) % 4, c, x)) for k in (1, 2, 3)}


def move(value, pairs):
    return lax.ppermute(value, AXES, pairs)


def split(a):
    high = a.astype(jnp.bfloat16)
    return high, (a - high.astype(F32)).astype(jnp.bfloat16)


def dot(a, b):
    return jnp.dot(a, b, preferred_element_type=F32)


def mm3(a, b):
    return dot(a[0], b[0]) + (dot(a[0], b[1]) + dot(a[1], b[0]))


def rows_times(row8, matrix):
    column = jnp.transpose(row8)[:, 0:1]
    product = (matrix * column).reshape(matrix.shape[0] // 8, 8, matrix.shape[1])
    total = jnp.sum(jnp.sum(product, axis=0), axis=0, keepdims=True)
    return jnp.broadcast_to(total, (8, matrix.shape[1]))


def block(i):
    return pl.ds(pl.multiple_of(i * B, B), B)


def place():
    tm = lax.axis_index("tm")
    return lax.axis_index("state"), lax.rem(tm // 2, 4), tm // 8, lax.rem(tm, 2)


def next_block(x, skip):
    one = lax.rem(x + 1, 4)
    return jnp.where(one == skip, lax.rem(x + 2, 4), one)


def pack_kernel(p_ref, r_ref, t_ref, m_ref, q_ref, pay0, pay1, pay2, pay3, local_ref, other_ref):
    x, _, _, c = place()
    for p, pay in enumerate((pay0, pay1, pay2, pay3)):
        j = lax.rem(x + p, 4)
        after = next_block(x, 2 * c + j // 2)
        for row, ref in ((0, p_ref), (B, r_ref)):
            pay[row : row + B, 0:B] = ref[j, :, block(x)]
            pay[row : row + B, B : 2 * B] = ref[j, :, block(after)]
        pay[256:320, 0:B] = t_ref[j, 0]
        pay[256:320, B : 2 * B] = t_ref[j, 1]
        pay[320:328, 0:B] = jnp.broadcast_to(m_ref[pl.ds(j, 1), :], (8, B))
        pay[320:328, B : 2 * B] = jnp.broadcast_to(q_ref[pl.ds(j, 1), :], (8, B))
    mine = 2 * lax.rem(x, 2) + c
    theirs = 2 * lax.rem(x, 2) + 1 - c
    local_ref[0:B, :] = p_ref[mine]
    local_ref[B : 2 * B, :] = r_ref[mine]
    other_ref[0:B, :] = p_ref[theirs]
    other_ref[B : 2 * B, :] = r_ref[theirs]


def step_kernel(ids_own, ids_other, pay0, pay1, pay2, pay3, local_ref, other_ref, out_ref, pf, rf, inc, vec):
    x, y, z, c = place()
    j = 2 * lax.rem(x, 2) + c
    same = (x // 2) == c
    low = lax.broadcasted_iota(jnp.int32, (64, B), 1) < 64
    for p, pay in enumerate((pay0, pay1, pay2, pay3)):
        source = lax.rem(j - p + 4, 4)
        after = next_block(source, x)
        for row, full in ((0, pf), (B, rf)):
            full[block(source), block(source)] = pay[row : row + B, 0:B]
            beside = pay[row : row + B, B : 2 * B]
            full[block(source), block(after)] = beside
            full[block(after), block(source)] = jnp.transpose(beside)
        for half in range(2):
            r = 2 * source + half
            at = j * 16 + r * 2
            first = jnp.where(same, ids_own[at], ids_other[at])
            second = jnp.where(same, ids_own[at + 1], ids_other[at + 1])
            tiles = pay[256:320, half * B : (half + 1) * B]
            turned = jnp.concatenate([tiles[:, 64:], tiles[:, :64]], axis=1)
            straight_to = jnp.where(low, first, second)
            turned_to = jnp.where(low, second, first)
            for g in range(4):
                here = jnp.where(low, 2 * g, 2 * g + 1)
                value = jnp.where(
                    straight_to == here, tiles, jnp.where(turned_to == here, turned, 0.0)
                )
                inc[pl.ds(pl.multiple_of(r * 64, 64), 64), g * B : (g + 1) * B] = value
        vec[0:8, block(source)] = pay[320:328, 0:B]
        vec[8:16, block(source)] = pay[320:328, B : 2 * B]
    for row, full in ((0, pf), (B, rf)):
        full[block(x), :] = jnp.where(
            same, local_ref[row : row + B, :], other_ref[row : row + B, :]
        )
        for d in (1, 2, 3):
            v = lax.rem(x + d, 4)
            full[block(v), block(x)] = jnp.transpose(full[block(x), block(v)])
    mixed = pf[...] + mm3(split(inc[...]), split(pf[...]))
    mixed = split(mixed)
    precision = split(rf[...])
    lead = split(mm3(split(vec[8:16, :]), precision))
    last = (z == NZ - 1) & (y == NY - 1) & (x == NX - 1) & (c == NC - 1)
    gain = mm3(precision, mixed)
    out_ref[0:W, :] = jnp.where(last, 0.0, gain)
    out_ref[W:FULL, :] = vec[0:8, :] - jnp.where(last, 0.0, mm3(lead, mixed))


def pair_kernel(own_ref, other_ref, out_ref):
    _, _, _, c = place()

    def compose(first, second):
        rows = jnp.concatenate(
            [first[pl.ds(pl.multiple_of(c * HALF, HALF), HALF), :], first[W:FULL, :]], axis=0
        )
        value = mm3(split(rows), split(second[0:W, :]))
        out_ref[0:HALF, :] = value[0:HALF]
        out_ref[HALF:PAN, :] = value[HALF:PAN] + second[W:FULL, :]

    @pl.when(c == 0)
    def _():
        compose(other_ref, own_ref)

    @pl.when(c == 1)
    def _():
        compose(own_ref, other_ref)


def fetch(panels, held, sems, index, c):
    copies = []
    for n, ref in enumerate(panels):
        k, mine = n // 2, n % 2
        half = c if mine == 0 else 1 - c
        slot = lax.rem(index - k + 4, 4)
        copy = pltpu.make_async_copy(ref, held.at[slot, half], sems.at[n])
        copy.start()
        copies.append(copy)
    return copies


def chain_kernel(along, whole, *refs):
    panels, out_ref, held, sems = refs[:8], refs[8], refs[9], refs[10]
    x, y, _, c = place()
    for copy in fetch(panels, held, sems, x if along == "x" else y, c):
        copy.wait()
    tail = held[3, 0, HALF:PAN, :]
    if whole:
        rows = jnp.concatenate([held[3, 0, 0:HALF, :], held[3, 1, 0:HALF, :], tail], axis=0)
    else:
        rows = jnp.concatenate([held[3, c, 0:HALF, :], tail], axis=0)
    size = W if whole else HALF
    for t in (2, 1, 0):
        left = split(rows)
        top = split(held[t, 0, 0:HALF, :])
        bottom = split(held[t, 1, 0:HALF, :])
        value = mm3((left[0][:, :HALF], left[1][:, :HALF]), top) + mm3(
            (left[0][:, HALF:], left[1][:, HALF:]), bottom
        )
        rows = jnp.concatenate([value[0:size], value[size:] + held[t, 0, HALF:PAN, :]], axis=0)
    out_ref[...] = rows


def plane_kernel(map_ref, carried_ref, came_ref, carried_out, out_ref):
    carried = carried_ref[...] + came_ref[...]
    carried_out[...] = carried
    out_ref[...] = rows_times(carried, map_ref[0:W, :]) + map_ref[W:FULL, :]


def down_kernel(carried_ref, came_ref, own_ref, other_ref, *refs):
    panels_y, panels_x = refs[0:8], refs[8:16]
    send0, send1, held_y, held_x, values, sems = refs[16:22]
    x, y, _, c = place()
    copies = fetch(panels_y, held_y, sems.at[0], y, c) + fetch(panels_x, held_x, sems.at[1], x, c)
    for copy in copies:
        copy.wait()
    carried = carried_ref[...] + came_ref[...]
    for held, index in ((held_y, y), (held_x, x)):
        for t in (3, 2, 1):
            matrix = jnp.concatenate([held[t, 0, 0:HALF, :], held[t, 1, 0:HALF, :]], axis=0)
            value = rows_times(carried, matrix) + held[t, 0, HALF:PAN, :]
            carried = jnp.where(t > index, value, carried)
    own_last = c == 1
    late = jnp.where(own_last, own_ref[...], other_ref[...])
    early = jnp.where(own_last, other_ref[...], own_ref[...])
    after = rows_times(carried, late[0:W]) + late[W:FULL]
    before = rows_times(after, early[0:W]) + early[W:FULL]
    top = lax.broadcasted_iota(jnp.int32, (8, W), 0) == 0
    values[...] = jnp.where(top, before, after)
    for r, send in enumerate((send0, send1)):
        send[...] = values[:, block(2 * c + lax.rem(x + r, 2))]


def shape(*dims):
    return jax.ShapeDtypeStruct(dims, F32)


PARAMS = pltpu.CompilerParams(vmem_limit_bytes=VMEM_LIMIT)
IN_VMEM = pl.BlockSpec(memory_space=pltpu.VMEM)
IN_SMEM = pl.BlockSpec(memory_space=pltpu.SMEM)
ANYWHERE = pl.BlockSpec(memory_space=pl.ANY)


def gather_panels(panel, shifts):
    panels = [panel, move(panel, SWAP)]
    for k in (1, 2, 3):
        came = move(panel, shifts[k])
        panels += [came, move(came, SWAP)]
    return panels


def chain(along, whole, panels):
    def kernel(*refs):
        chain_kernel(along, whole, *refs)

    return pl.pallas_call(
        kernel,
        out_shape=shape(FULL if whole else PAN, W),
        in_specs=[ANYWHERE] * 8,
        out_specs=IN_VMEM,
        scratch_shapes=[pltpu.VMEM((4, 2, PAN, W), F32), pltpu.SemaphoreType.DMA((8,))],
        compiler_params=PARAMS,
        name="chain_" + along,
    )(*panels)


def on_device(spread, inverse, tiles, ids, mean, prior):
    ids_own = ids.reshape(-1)
    ids_other = move(ids_own, SWAP)
    *pays, local, other = pl.pallas_call(
        pack_kernel,
        out_shape=[shape(328, HALF)] * 4 + [shape(2 * B, W)] * 2,
        in_specs=[IN_VMEM] * 5,
        out_specs=[IN_VMEM] * 6,
        compiler_params=PARAMS,
        name="pack",
    )(spread, inverse, tiles, mean, prior)
    got = [move(pay, SPREAD[p]) for p, pay in enumerate(pays)]
    other = move(other, SWAP)
    step = pl.pallas_call(
        step_kernel,
        out_shape=shape(FULL, W),
        in_specs=[IN_SMEM] * 2 + [IN_VMEM] * 6,
        out_specs=IN_VMEM,
        scratch_shapes=[pltpu.VMEM((W, W), F32)] * 3 + [pltpu.VMEM((16, W), F32)],
        compiler_params=PARAMS,
        name="step",
    )(ids_own, ids_other, *got, local, other)
    twin = move(step, SWAP)
    pair = pl.pallas_call(
        pair_kernel,
        out_shape=shape(PAN, W),
        in_specs=[IN_VMEM] * 2,
        out_specs=IN_VMEM,
        compiler_params=PARAMS,
        name="pair",
    )(step, twin)
    panels_x = gather_panels(pair, SHIFT_X)
    row_map = chain("x", False, panels_x)
    panels_y = gather_panels(row_map, SHIFT_Y)
    plane_map = chain("y", True, panels_y)
    carried = jnp.zeros((8, W), F32)
    came = jnp.zeros((8, W), F32)
    for i in range(NZ - 1):
        carried, out = pl.pallas_call(
            plane_kernel,
            out_shape=[shape(8, W)] * 2,
            in_specs=[IN_VMEM] * 3,
            out_specs=[IN_VMEM] * 2,
            compiler_params=PARAMS,
            name="plane",
        )(plane_map, carried, came)
        came = lax.ppermute(out, "tm", [(t, t - 8) for t in range(64) if t // 8 == 7 - i])
    sends = pl.pallas_call(
        down_kernel,
        out_shape=[shape(8, B)] * 2,
        in_specs=[IN_VMEM] * 4 + [ANYWHERE] * 16,
        out_specs=[IN_VMEM] * 2,
        scratch_shapes=[pltpu.VMEM((4, 2, PAN, W), F32)] * 2
        + [pltpu.VMEM((8, W), F32), pltpu.SemaphoreType.DMA((2, 8))],
        compiler_params=PARAMS,
        name="down",
    )(carried, came, step, twin, *panels_y, *panels_x)
    even, odd = (move(send, COLLECT[r])[0:2] for r, send in enumerate(sends))
    flip = lax.rem(lax.axis_index("state"), 2) == 1
    return jnp.concatenate([jnp.where(flip, odd, even), jnp.where(flip, even, odd)], axis=0)


def solution(mesh):
    return jax.shard_map(
        on_device,
        mesh=mesh,
        in_specs=(
            P("tm", "state", None),
            P("tm", "state", None),
            P("tm", "state", None, None),
            P("tm", None, None),
            P("tm", "state"),
            P("tm", "state"),
        ),
        out_specs=P("tm", "state"),
        check_vma=False,
    )
```

```python
import jax
import jax.numpy as jnp
from jax import lax
from jax.experimental import pallas as pl
from jax.experimental.pallas import tpu as pltpu
from jax.sharding import PartitionSpec as P

NZ, NY, NC, NX = 8, 4, 2, 4
W = 512
B = 128
HALF = 256
PAN = HALF + 8
LOW = B + 8
FULL = W + 8
AXES = ("tm", "state")
F32 = jnp.float32
VMEM_LIMIT = 24 * 1024 * 1024


def joint(move):
    pairs = []
    for z in range(NZ):
        for y in range(NY):
            for c in range(NC):
                for x in range(NX):
                    y2, c2, x2 = move(y, c, x)
                    source = ((z * NY + y) * NC + c) * NX + x
                    pairs.append((source, ((z * NY + y2) * NC + c2) * NX + x2))
    return pairs


def spread_move(p):
    def move(y, c, x):
        q = (x + p) % 4
        return y, q % 2, 2 * c + q // 2

    return move


def collect_move(r):
    def move(y, c, x):
        return y, x // 2, 2 * c + (x + r) % 2

    return move


SWAP = joint(lambda y, c, x: (y, 1 - c, x))
SPREAD = [joint(spread_move(p)) for p in range(4)]
COLLECT = [joint(collect_move(r)) for r in range(2)]
SHIFT_X = {k: joint(lambda y, c, x, k=k: (y, c, (x + k) % 4)) for k in (1, 2, 3)}
SHIFT_Y = {k: joint(lambda y, c, x, k=k: ((y + k) % 4, c, x)) for k in (1, 2, 3)}


def move(value, pairs):
    return lax.ppermute(value, AXES, pairs)


def split(a):
    high = a.astype(jnp.bfloat16)
    return high, (a - high.astype(F32)).astype(jnp.bfloat16)


def dot(a, b):
    return jnp.dot(a, b, preferred_element_type=F32)


def mm3(a, b):
    return dot(a[0], b[0]) + (dot(a[0], b[1]) + dot(a[1], b[0]))


def rows_times(row8, matrix):
    column = jnp.transpose(row8)[:, 0:1]
    product = (matrix * column).reshape(matrix.shape[0] // 8, 8, matrix.shape[1])
    total = jnp.sum(jnp.sum(product, axis=0), axis=0, keepdims=True)
    return jnp.broadcast_to(total, (8, matrix.shape[1]))


def block(i):
    return pl.ds(pl.multiple_of(i * B, B), B)


def place():
    tm = lax.axis_index("tm")
    return lax.axis_index("state"), lax.rem(tm // 2, 4), tm // 8, lax.rem(tm, 2)


def next_block(x, skip):
    one = lax.rem(x + 1, 4)
    return jnp.where(one == skip, lax.rem(x + 2, 4), one)


def pack_kernel(p_ref, r_ref, t_ref, m_ref, q_ref, pay0, pay1, pay2, pay3, local_ref, other_ref, means, sems):
    x, _, _, c = place()
    copies = []

    def start(source, target):
        copy = pltpu.make_async_copy(source, target, sems.at[len(copies)])
        copy.start()
        copies.append(copy)

    start(m_ref, means.at[0])
    start(q_ref, means.at[1])
    for p, pay in enumerate((pay0, pay1, pay2, pay3)):
        j = lax.rem(x + p, 4)
        after = next_block(x, 2 * c + j // 2)
        for row, ref in ((0, p_ref), (B, r_ref)):
            start(ref.at[j, :, block(x)], pay.at[row : row + B, 0:B])
            start(ref.at[j, :, block(after)], pay.at[row : row + B, B : 2 * B])
        start(t_ref.at[j, 0], pay.at[256:320, 0:B])
        start(t_ref.at[j, 1], pay.at[256:320, B : 2 * B])
    mine = 2 * lax.rem(x, 2) + c
    theirs = 2 * lax.rem(x, 2) + 1 - c
    for row, ref in ((0, p_ref), (B, r_ref)):
        start(ref.at[mine], local_ref.at[row : row + B])
        start(ref.at[theirs], other_ref.at[row : row + B])
    copies[0].wait()
    copies[1].wait()
    for p, pay in enumerate((pay0, pay1, pay2, pay3)):
        j = lax.rem(x + p, 4)
        pay[320:328, 0:B] = jnp.broadcast_to(means[0, pl.ds(j, 1), :], (8, B))
        pay[320:328, B : 2 * B] = jnp.broadcast_to(means[1, pl.ds(j, 1), :], (8, B))
    for copy in copies[2:]:
        copy.wait()


def step_kernel(ids_own, ids_other, pay0, pay1, pay2, pay3, local_ref, other_ref, out_ref, pf, rf, inc, vec):
    x, y, z, c = place()
    j = 2 * lax.rem(x, 2) + c
    same = (x // 2) == c
    low = lax.broadcasted_iota(jnp.int32, (64, B), 1) < 64
    for p, pay in enumerate((pay0, pay1, pay2, pay3)):
        source = lax.rem(j - p + 4, 4)
        after = next_block(source, x)
        for row, full in ((0, pf), (B, rf)):
            full[block(source), block(source)] = pay[row : row + B, 0:B]
            beside = pay[row : row + B, B : 2 * B]
            full[block(source), block(after)] = beside
            full[block(after), block(source)] = jnp.transpose(beside)
        for half in range(2):
            r = 2 * source + half
            at = j * 16 + r * 2
            first = jnp.where(same, ids_own[at], ids_other[at])
            second = jnp.where(same, ids_own[at + 1], ids_other[at + 1])
            tiles = pay[256:320, half * B : (half + 1) * B]
            turned = jnp.concatenate([tiles[:, 64:], tiles[:, :64]], axis=1)
            straight_to = jnp.where(low, first, second)
            turned_to = jnp.where(low, second, first)
            for g in range(4):
                here = jnp.where(low, 2 * g, 2 * g + 1)
                value = jnp.where(
                    straight_to == here, tiles, jnp.where(turned_to == here, turned, 0.0)
                )
                inc[pl.ds(pl.multiple_of(r * 64, 64), 64), g * B : (g + 1) * B] = value
        vec[0:8, block(source)] = pay[320:328, 0:B]
        vec[8:16, block(source)] = pay[320:328, B : 2 * B]
    for row, full in ((0, pf), (B, rf)):
        full[block(x), :] = jnp.where(
            same, local_ref[row : row + B, :], other_ref[row : row + B, :]
        )
        for d in (1, 2, 3):
            v = lax.rem(x + d, 4)
            full[block(v), block(x)] = jnp.transpose(full[block(x), block(v)])
    mixed = pf[...] + mm3(split(inc[...]), split(pf[...]))
    mixed = split(mixed)
    precision = split(rf[...])
    lead = split(mm3(split(vec[8:16, :]), precision))
    last = (z == NZ - 1) & (y == NY - 1) & (x == NX - 1) & (c == NC - 1)
    gain = mm3(precision, mixed)
    out_ref[0:W, :] = jnp.where(last, 0.0, gain)
    out_ref[W:FULL, :] = vec[0:8, :] - jnp.where(last, 0.0, mm3(lead, mixed))


def pair_kernel(own_ref, other_ref, top_ref, low_ref):
    _, _, _, c = place()

    def compose(first, second):
        rows = jnp.concatenate(
            [first[pl.ds(pl.multiple_of(c * HALF, HALF), HALF), :], first[W:FULL, :]], axis=0
        )
        value = mm3(split(rows), split(second[0:W, :]))
        top_ref[...] = value[0:B]
        low_ref[0:B, :] = value[B:HALF]
        low_ref[B:LOW, :] = value[HALF:PAN] + second[W:FULL, :]

    @pl.when(c == 0)
    def _():
        compose(other_ref, own_ref)

    @pl.when(c == 1)
    def _():
        compose(own_ref, other_ref)


def fetch(panels, held, sems, index, c):
    copies = []
    for n, ref in enumerate(panels):
        k, mine, low = n // 4, n // 2 % 2, n % 2
        half = c if mine == 0 else 1 - c
        slot = lax.rem(index - k + 4, 4)
        rows = pl.ds(B, LOW) if low else pl.ds(0, B)
        copy = pltpu.make_async_copy(ref, held.at[slot, half, rows], sems.at[n])
        copy.start()
        copies.append(copy)
    return copies


def chain_kernel(along, whole, *refs):
    panels, outs, held, sems = refs[:16], refs[16:-2], refs[-2], refs[-1]
    x, y, _, c = place()
    for copy in fetch(panels, held, sems, x if along == "x" else y, c):
        copy.wait()
    tail = held[3, 0, HALF:PAN, :]
    if whole:
        rows = jnp.concatenate([held[3, 0, 0:HALF, :], held[3, 1, 0:HALF, :], tail], axis=0)
    else:
        rows = jnp.concatenate([held[3, c, 0:HALF, :], tail], axis=0)
    size = W if whole else HALF
    for t in (2, 1, 0):
        left = split(rows)
        top = split(held[t, 0, 0:HALF, :])
        bottom = split(held[t, 1, 0:HALF, :])
        value = mm3((left[0][:, :HALF], left[1][:, :HALF]), top) + mm3(
            (left[0][:, HALF:], left[1][:, HALF:]), bottom
        )
        rows = jnp.concatenate([value[0:size], value[size:] + held[t, 0, HALF:PAN, :]], axis=0)
    if whole:
        outs[0][...] = rows
    else:
        outs[0][...] = rows[0:B]
        outs[1][...] = rows[B:]


def plane_kernel(map_ref, carried_ref, came_ref, carried_out, out_ref):
    carried = carried_ref[...] + came_ref[...]
    carried_out[...] = carried
    out_ref[...] = rows_times(carried, map_ref[0:W, :]) + map_ref[W:FULL, :]


def down_kernel(carried_ref, came_ref, own_ref, other_ref, *refs):
    panels_y, panels_x = refs[0:16], refs[16:32]
    send0, send1, held_y, held_x, values, sems = refs[32:38]
    x, y, _, c = place()
    copies = fetch(panels_y, held_y, sems.at[0], y, c) + fetch(panels_x, held_x, sems.at[1], x, c)
    for copy in copies:
        copy.wait()
    carried = carried_ref[...] + came_ref[...]
    for held, index in ((held_y, y), (held_x, x)):
        for t in (3, 2, 1):
            matrix = jnp.concatenate([held[t, 0, 0:HALF, :], held[t, 1, 0:HALF, :]], axis=0)
            value = rows_times(carried, matrix) + held[t, 0, HALF:PAN, :]
            carried = jnp.where(t > index, value, carried)
    own_last = c == 1
    late = jnp.where(own_last, own_ref[...], other_ref[...])
    early = jnp.where(own_last, other_ref[...], own_ref[...])
    after = rows_times(carried, late[0:W]) + late[W:FULL]
    before = rows_times(after, early[0:W]) + early[W:FULL]
    top = lax.broadcasted_iota(jnp.int32, (8, W), 0) == 0
    values[...] = jnp.where(top, before, after)
    for r, send in enumerate((send0, send1)):
        send[...] = values[:, block(2 * c + lax.rem(x + r, 2))]


def shape(*dims):
    return jax.ShapeDtypeStruct(dims, F32)


PARAMS = pltpu.CompilerParams(vmem_limit_bytes=VMEM_LIMIT)
IN_VMEM = pl.BlockSpec(memory_space=pltpu.VMEM)
IN_SMEM = pl.BlockSpec(memory_space=pltpu.SMEM)
IN_HBM = pl.BlockSpec(memory_space=pltpu.HBM)
ANYWHERE = pl.BlockSpec(memory_space=pl.ANY)


def both(value):
    return [value, move(value, SWAP)]


def gather_panels(top, low, shifts):
    left_top, right_low = move(top, shifts[1]), move(low, shifts[3])
    left_low, right_top = move(low, shifts[1]), move(top, shifts[3])
    far_top, far_low = move(left_top, shifts[1]), move(right_low, shifts[3])
    panels = []
    for pair in ((top, low), (left_top, left_low), (far_top, far_low), (right_top, right_low)):
        own, other = zip(*(both(value) for value in pair))
        panels += [*own, *other]
    return panels


def chain(along, whole, panels):
    def kernel(*refs):
        chain_kernel(along, whole, *refs)

    return pl.pallas_call(
        kernel,
        out_shape=shape(FULL, W) if whole else [shape(B, W), shape(LOW, W)],
        in_specs=[ANYWHERE] * 16,
        out_specs=IN_VMEM if whole else [IN_VMEM] * 2,
        scratch_shapes=[pltpu.VMEM((4, 2, PAN, W), F32), pltpu.SemaphoreType.DMA((16,))],
        compiler_params=PARAMS,
        name="chain_" + along,
    )(*panels)


def in_hbm(value):
    return pltpu.with_memory_space_constraint(value, pltpu.HBM)


def on_device(spread, inverse, tiles, ids, mean, prior):
    ids_own = ids.reshape(-1)
    ids_other = move(ids_own, SWAP)
    *pays, local, other = pl.pallas_call(
        pack_kernel,
        out_shape=[shape(328, HALF)] * 4 + [shape(2 * B, W)] * 2,
        in_specs=[IN_HBM] * 5,
        out_specs=[IN_VMEM] * 6,
        scratch_shapes=[pltpu.VMEM((2, 4, B), F32), pltpu.SemaphoreType.DMA((30,))],
        compiler_params=PARAMS,
        name="pack",
    )(*(in_hbm(a) for a in (spread, inverse, tiles, mean, prior)))
    got = [move(pay, SPREAD[p]) for p, pay in enumerate(pays)]
    other = move(other, SWAP)
    step = pl.pallas_call(
        step_kernel,
        out_shape=shape(FULL, W),
        in_specs=[IN_SMEM] * 2 + [IN_VMEM] * 6,
        out_specs=IN_VMEM,
        scratch_shapes=[pltpu.VMEM((W, W), F32)] * 3 + [pltpu.VMEM((16, W), F32)],
        compiler_params=PARAMS,
        name="step",
    )(ids_own, ids_other, *got, local, other)
    twin = move(step, SWAP)
    pair = pl.pallas_call(
        pair_kernel,
        out_shape=[shape(B, W), shape(LOW, W)],
        in_specs=[IN_VMEM] * 2,
        out_specs=[IN_VMEM] * 2,
        compiler_params=PARAMS,
        name="pair",
    )(step, twin)
    panels_x = gather_panels(*pair, SHIFT_X)
    row_map = chain("x", False, panels_x)
    panels_y = gather_panels(*row_map, SHIFT_Y)
    plane_map = chain("y", True, panels_y)
    carried = jnp.zeros((8, W), F32)
    came = jnp.zeros((8, W), F32)
    for i in range(NZ - 1):
        carried, out = pl.pallas_call(
            plane_kernel,
            out_shape=[shape(8, W)] * 2,
            in_specs=[IN_VMEM] * 3,
            out_specs=[IN_VMEM] * 2,
            compiler_params=PARAMS,
            name="plane",
        )(plane_map, carried, came)
        came = lax.ppermute(out, "tm", [(t, t - 8) for t in range(64) if t // 8 == 7 - i])
    sends = pl.pallas_call(
        down_kernel,
        out_shape=[shape(8, B)] * 2,
        in_specs=[IN_VMEM] * 4 + [ANYWHERE] * 32,
        out_specs=[IN_VMEM] * 2,
        scratch_shapes=[pltpu.VMEM((4, 2, PAN, W), F32)] * 2
        + [pltpu.VMEM((8, W), F32), pltpu.SemaphoreType.DMA((2, 16))],
        compiler_params=PARAMS,
        name="down",
    )(carried, came, step, twin, *panels_y, *panels_x)
    even, odd = (move(send, COLLECT[r])[0:2] for r, send in enumerate(sends))
    flip = lax.rem(lax.axis_index("state"), 2) == 1
    return jnp.concatenate([jnp.where(flip, odd, even), jnp.where(flip, even, odd)], axis=0)


def solution(mesh):
    return jax.shard_map(
        on_device,
        mesh=mesh,
        in_specs=(
            P("tm", "state", None),
            P("tm", "state", None),
            P("tm", "state", None, None),
            P("tm", None, None),
            P("tm", "state"),
            P("tm", "state"),
        ),
        out_specs=P("tm", "state"),
        check_vma=False,
    )
```

```python
import jax
import jax.numpy as jnp
from jax import lax
from jax.experimental import pallas as pl
from jax.experimental.pallas import tpu as pltpu
from jax.sharding import PartitionSpec as P

NZ, NY, NC, NX = 8, 4, 2, 4
W = 512
B = 128
HALF = 256
PAN = HALF + 8
FULL = W + 8
AXES = ("tm", "state")
F32 = jnp.float32
VMEM_LIMIT = 24 * 1024 * 1024


def turn(x):
    return 2 * (x % 2) + x // 2


def joint(move):
    pairs = []
    for z in range(NZ):
        for y in range(NY):
            for c in range(NC):
                for x in range(NX):
                    y2, c2, x2 = move(y, c, x)
                    source = ((z * NY + y) * NC + c) * NX + x
                    pairs.append((source, ((z * NY + y2) * NC + c2) * NX + x2))
    return pairs


def spread_move(p):
    def move(y, c, x):
        q = (x + p) % 4
        return y, q % 2, turn(2 * c + q // 2)

    return move


def collect_move(r):
    def move(y, c, x):
        return y, x % 2, 2 * c + (x // 2 + r) % 2

    return move


SWAP = joint(lambda y, c, x: (y, 1 - c, x))
SPREAD = [joint(spread_move(p)) for p in range(4)]
COLLECT = [joint(collect_move(r)) for r in range(2)]
RING_X = joint(lambda y, c, x: (y, c, (x + 1 + 2 * c) % 4))
RING_Y = joint(lambda y, c, x: ((y + 1 + 2 * c) % 4, c, x))


def move(value, pairs):
    return lax.ppermute(value, AXES, pairs)


def split(a):
    high = a.astype(jnp.bfloat16)
    return high, (a - high.astype(F32)).astype(jnp.bfloat16)


def dot(a, b):
    return jnp.dot(a, b, preferred_element_type=F32)


def mm3(a, b):
    return dot(a[0], b[0]) + (dot(a[0], b[1]) + dot(a[1], b[0]))


def rows_times(row8, matrix):
    column = jnp.transpose(row8)[:, 0:1]
    product = (matrix * column).reshape(matrix.shape[0] // 8, 8, matrix.shape[1])
    total = jnp.sum(jnp.sum(product, axis=0), axis=0, keepdims=True)
    return jnp.broadcast_to(total, (8, matrix.shape[1]))


def block(i):
    return pl.ds(pl.multiple_of(i * B, B), B)


def place():
    tm = lax.axis_index("tm")
    return lax.axis_index("state"), lax.rem(tm // 2, 4), tm // 8, lax.rem(tm, 2)


def next_block(x, skip):
    one = lax.rem(x + 1, 4)
    return jnp.where(one == skip, lax.rem(x + 2, 4), one)


def pack_kernel(
    p_ref, r_ref, t_ref, m_ref, q_ref, i_ref, pay0, pay1, pay2, pay3, local_ref, other_ref, means, ids, sems
):
    x, _, _, c = place()
    copies = []

    def start(source, target):
        copy = pltpu.make_async_copy(source, target, sems.at[len(copies)])
        copy.start()
        copies.append(copy)

    start(m_ref, means.at[0])
    start(q_ref, means.at[1])
    start(i_ref, ids)
    for p, pay in enumerate((pay0, pay1, pay2, pay3)):
        j = lax.rem(x + p, 4)
        after = next_block(x, 2 * lax.rem(j // 2, 2) + c)
        for row, ref in ((0, p_ref), (B, r_ref)):
            start(ref.at[j, :, block(x)], pay.at[row : row + B, 0:B])
            start(ref.at[j, :, block(after)], pay.at[row : row + B, B : 2 * B])
        start(t_ref.at[j, 0], pay.at[256:320, 0:B])
        start(t_ref.at[j, 1], pay.at[256:320, B : 2 * B])
    mine = 2 * (x // 2) + c
    theirs = 2 * (x // 2) + 1 - c
    for row, ref in ((0, p_ref), (B, r_ref)):
        start(ref.at[mine], local_ref.at[row : row + B])
        start(ref.at[theirs], other_ref.at[row : row + B])
    for copy in copies[:3]:
        copy.wait()
    lane = lax.broadcasted_iota(jnp.int32, (2, 8), 1)
    low = lax.broadcasted_iota(jnp.int32, (1, B), 1) < 64
    for p, pay in enumerate((pay0, pay1, pay2, pay3)):
        j = lax.rem(x + p, 4)
        pay[320:321, 0:B] = means[0, pl.ds(j, 1), :]
        pay[320:321, B : 2 * B] = means[1, pl.ds(j, 1), :]
        for half in range(2):
            pair = jnp.sum(
                jnp.where(lane == 2 * x + half, ids[j].astype(F32), 0.0), axis=1, keepdims=True
            )
            first = jnp.broadcast_to(pair[0:1], (1, B))
            second = jnp.broadcast_to(pair[1:2], (1, B))
            pay[321:322, half * B : (half + 1) * B] = jnp.where(low, first, second)
            pay[322:323, half * B : (half + 1) * B] = jnp.where(low, second, first)
    for copy in copies[3:]:
        copy.wait()


def step_kernel(pay0, pay1, pay2, pay3, local_ref, other_ref, out_ref, pf, rf, inc, vec):
    x, y, z, c = place()
    j = 2 * (x // 2) + c
    same = lax.rem(x, 2) == c
    low = lax.broadcasted_iota(jnp.int32, (64, B), 1) < 64
    for p, pay in enumerate((pay0, pay1, pay2, pay3)):
        source = lax.rem(j - p + 4, 4)
        after = next_block(source, x)
        for row, full in ((0, pf), (B, rf)):
            full[block(source), block(source)] = pay[row : row + B, 0:B]
            beside = pay[row : row + B, B : 2 * B]
            full[block(source), block(after)] = beside
            full[block(after), block(source)] = jnp.transpose(beside)
        for half in range(2):
            r = 2 * source + half
            lanes = slice(half * B, (half + 1) * B)
            tiles = pay[256:320, lanes]
            turned = jnp.concatenate([tiles[:, 64:], tiles[:, :64]], axis=1)
            straight_to = jnp.broadcast_to(pay[321:322, lanes], (64, B))
            turned_to = jnp.broadcast_to(pay[322:323, lanes], (64, B))
            for g in range(4):
                here = jnp.where(low, 2.0 * g, 2.0 * g + 1.0)
                value = jnp.where(
                    straight_to == here, tiles, jnp.where(turned_to == here, turned, 0.0)
                )
                inc[pl.ds(pl.multiple_of(r * 64, 64), 64), g * B : (g + 1) * B] = value
        vec[0:8, block(source)] = jnp.broadcast_to(pay[320:321, 0:B], (8, B))
        vec[8:16, block(source)] = jnp.broadcast_to(pay[320:321, B : 2 * B], (8, B))
    for row, full in ((0, pf), (B, rf)):
        full[block(x), :] = jnp.where(
            same, local_ref[row : row + B, :], other_ref[row : row + B, :]
        )
        for d in (1, 2, 3):
            v = lax.rem(x + d, 4)
            full[block(v), block(x)] = jnp.transpose(full[block(x), block(v)])
    mixed = pf[...] + mm3(split(inc[...]), split(pf[...]))
    mixed = split(mixed)
    precision = split(rf[...])
    lead = split(mm3(split(vec[8:16, :]), precision))
    last = (z == NZ - 1) & (y == NY - 1) & (x == NX - 1) & (c == NC - 1)
    gain = mm3(precision, mixed)
    out_ref[0:W, :] = jnp.where(last, 0.0, gain)
    out_ref[W:FULL, :] = vec[0:8, :] - jnp.where(last, 0.0, mm3(lead, mixed))


def halves(ref, c):
    n = pl.multiple_of(c * HALF, HALF)
    m = pl.multiple_of((1 - c) * HALF, HALF)
    return ref[pl.ds(n, HALF), :], ref[pl.ds(m, HALF), :]


def pair_kernel(own_ref, other_ref, first_ref, second_ref):
    _, _, _, c = place()

    def compose(early, late):
        rows = jnp.concatenate([*halves(early, c), early[W:FULL, :]], axis=0)
        value = mm3(split(rows), split(late[0:W, :]))
        tail = value[W:] + late[W:FULL, :]
        for n, ref in enumerate((first_ref, second_ref)):
            ref[0:HALF, :] = value[n * HALF : (n + 1) * HALF]
            ref[HALF:PAN, :] = tail

    @pl.when(c == 0)
    def _():
        compose(other_ref, own_ref)

    @pl.when(c == 1)
    def _():
        compose(own_ref, other_ref)


def fetch(panels, held, sems, index, c, turned):
    forth, back, far = index + 3 - 2 * c, index + 1 + 2 * c, index + 2
    homes = ((index, c), (index, 1 - c), (forth, c), (forth, 1 - c), (back, 1 - c), (back, c), (far, c), (far, 1 - c))
    copies = []
    for n, (ref, (source, half)) in enumerate(zip(panels, homes)):
        slot = lax.rem(source, 4)
        if turned:
            slot = 2 * lax.rem(slot, 2) + slot // 2
        copy = pltpu.make_async_copy(ref, held.at[slot, half], sems.at[n])
        copy.start()
        copies.append(copy)
    return copies


def chain_kernel(along, whole, *refs):
    panels, held, outs, sems = refs[:8], refs[8], refs[9:-1], refs[-1]
    x, y, _, c = place()
    for copy in fetch(panels, held, sems, x if along == "x" else y, c, along == "x"):
        copy.wait()
    tail = held[3, 0, HALF:PAN, :]
    begin = 0 if whole else c
    rows = jnp.concatenate([held[3, begin, 0:HALF, :], held[3, 1 - begin, 0:HALF, :], tail], axis=0)
    for t in (2, 1, 0):
        left = split(rows)
        top = split(held[t, 0, 0:HALF, :])
        bottom = split(held[t, 1, 0:HALF, :])
        value = mm3((left[0][:, :HALF], left[1][:, :HALF]), top) + mm3(
            (left[0][:, HALF:], left[1][:, HALF:]), bottom
        )
        rows = jnp.concatenate([value[0:W], value[W:] + held[t, 0, HALF:PAN, :]], axis=0)
    if whole:
        outs[0][...] = rows
    else:
        for n in range(2):
            outs[n][0:HALF, :] = rows[n * HALF : (n + 1) * HALF]
            outs[n][HALF:PAN, :] = rows[W:FULL]


def plane_kernel(map_ref, carried_ref, came_ref, carried_out, out_ref):
    carried = carried_ref[...] + came_ref[...]
    carried_out[...] = carried
    out_ref[...] = rows_times(carried, map_ref[0:W, :]) + map_ref[W:FULL, :]


def down_kernel(carried_ref, came_ref, own_ref, other_ref, held_y, held_x, send0, send1, values):
    x, y, _, c = place()
    carried = carried_ref[...] + came_ref[...]
    for held, index in ((held_y, y), (held_x, 2 * lax.rem(x, 2) + x // 2)):
        for t in (3, 2, 1):
            matrix = jnp.concatenate([held[t, 0, 0:HALF, :], held[t, 1, 0:HALF, :]], axis=0)
            value = rows_times(carried, matrix) + held[t, 0, HALF:PAN, :]
            carried = jnp.where(t > index, value, carried)
    own_last = c == 1
    late = jnp.where(own_last, own_ref[...], other_ref[...])
    early = jnp.where(own_last, other_ref[...], own_ref[...])
    after = rows_times(carried, late[0:W]) + late[W:FULL]
    before = rows_times(after, early[0:W]) + early[W:FULL]
    top = lax.broadcasted_iota(jnp.int32, (8, W), 0) == 0
    values[...] = jnp.where(top, before, after)
    for r, send in enumerate((send0, send1)):
        send[...] = values[:, block(2 * c + lax.rem(x // 2 + r, 2))]


def shape(*dims):
    return jax.ShapeDtypeStruct(dims, F32)


PARAMS = pltpu.CompilerParams(vmem_limit_bytes=VMEM_LIMIT)
IN_VMEM = pl.BlockSpec(memory_space=pltpu.VMEM)
IN_HBM = pl.BlockSpec(memory_space=pltpu.HBM)
ANYWHERE = pl.BlockSpec(memory_space=pl.ANY)


def gather_panels(first, second, ring):
    one, two = move(first, ring), move(second, ring)
    far = move(one, ring)
    return first, second, one, two, move(one, SWAP), move(two, SWAP), far, move(far, SWAP)


def chain(along, whole, panels):
    def kernel(*refs):
        chain_kernel(along, whole, *refs)

    return pl.pallas_call(
        kernel,
        out_shape=[shape(4, 2, PAN, W)]
        + ([shape(FULL, W)] if whole else [shape(PAN, W)] * 2),
        in_specs=[ANYWHERE] * 8,
        out_specs=[IN_VMEM] * (2 if whole else 3),
        scratch_shapes=[pltpu.SemaphoreType.DMA((8,))],
        compiler_params=PARAMS,
        name="chain_" + along,
    )(*panels)


def in_hbm(value):
    return pltpu.with_memory_space_constraint(value, pltpu.HBM)


def on_device(spread, inverse, tiles, ids, mean, prior):
    *pays, local, other = pl.pallas_call(
        pack_kernel,
        out_shape=[shape(328, HALF)] * 4 + [shape(2 * B, W)] * 2,
        in_specs=[IN_HBM] * 6,
        out_specs=[IN_VMEM] * 6,
        scratch_shapes=[
            pltpu.VMEM((2, 4, B), F32),
            pltpu.VMEM((4, 2, 8), jnp.int32),
            pltpu.SemaphoreType.DMA((31,)),
        ],
        compiler_params=PARAMS,
        name="pack",
    )(*(in_hbm(a) for a in (spread, inverse, tiles, mean, prior, jnp.swapaxes(ids, 1, 2))))
    got = [move(pay, SPREAD[p]) for p, pay in enumerate(pays)]
    other = move(other, SWAP)
    step = pl.pallas_call(
        step_kernel,
        out_shape=shape(FULL, W),
        in_specs=[IN_VMEM] * 6,
        out_specs=IN_VMEM,
        scratch_shapes=[pltpu.VMEM((W, W), F32)] * 3 + [pltpu.VMEM((16, W), F32)],
        compiler_params=PARAMS,
        name="step",
    )(*got, local, other)
    twin = move(step, SWAP)
    pair = pl.pallas_call(
        pair_kernel,
        out_shape=[shape(PAN, W)] * 2,
        in_specs=[IN_VMEM] * 2,
        out_specs=[IN_VMEM] * 2,
        compiler_params=PARAMS,
        name="pair",
    )(step, twin)
    held_x, *row_map = chain("x", False, gather_panels(*pair, RING_X))
    held_y, plane_map = chain("y", True, gather_panels(*row_map, RING_Y))
    carried = jnp.zeros((8, W), F32)
    came = jnp.zeros((8, W), F32)
    for i in range(NZ - 1):
        carried, out = pl.pallas_call(
            plane_kernel,
            out_shape=[shape(8, W)] * 2,
            in_specs=[IN_VMEM] * 3,
            out_specs=[IN_VMEM] * 2,
            compiler_params=PARAMS,
            name="plane",
        )(plane_map, carried, came)
        came = lax.ppermute(out, "tm", [(t, t - 8) for t in range(64) if t // 8 == 7 - i and t % 2])
    carried = carried + came
    came = lax.ppermute(carried, "tm", [(t, t - 1) for t in range(64) if t % 2])
    sends = pl.pallas_call(
        down_kernel,
        out_shape=[shape(8, B)] * 2,
        in_specs=[IN_VMEM] * 6,
        out_specs=[IN_VMEM] * 2,
        scratch_shapes=[pltpu.VMEM((8, W), F32)],
        compiler_params=PARAMS,
        name="down",
    )(carried, came, step, twin, held_y, held_x)
    even, odd = (move(send, COLLECT[r])[0:2] for r, send in enumerate(sends))
    flip = lax.rem(lax.axis_index("state"), 2) == 1
    return jnp.concatenate([jnp.where(flip, odd, even), jnp.where(flip, even, odd)], axis=0)


def solution(mesh):
    return jax.shard_map(
        on_device,
        mesh=mesh,
        in_specs=(
            P("tm", "state", None),
            P("tm", "state", None),
            P("tm", "state", None, None),
            P("tm", None, None),
            P("tm", "state"),
            P("tm", "state"),
        ),
        out_specs=P("tm", "state"),
        check_vma=False,
    )
```

```python
import jax
import jax.numpy as jnp
from jax import lax
from jax.experimental import pallas as pl
from jax.experimental.pallas import tpu as pltpu
from jax.sharding import PartitionSpec as P

NZ, NY, NC, NX = 8, 4, 2, 4
W = 512
B = 128
HALF = 256
PAN = HALF + 8
FULL = W + 8
AXES = ("tm", "state")
F32 = jnp.float32
VMEM_LIMIT = 24 * 1024 * 1024


def turn(x):
    return 2 * (x % 2) + x // 2


def joint(move):
    pairs = []
    for z in range(NZ):
        for y in range(NY):
            for c in range(NC):
                for x in range(NX):
                    y2, c2, x2 = move(y, c, x)
                    source = ((z * NY + y) * NC + c) * NX + x
                    pairs.append((source, ((z * NY + y2) * NC + c2) * NX + x2))
    return pairs


def spread_move(p):
    def move(y, c, x):
        q = (x + p) % 4
        return y, q % 2, turn(2 * c + q // 2)

    return move


def collect_move(r):
    def move(y, c, x):
        return y, x % 2, 2 * c + (x // 2 + r) % 2

    return move


SWAP = joint(lambda y, c, x: (y, 1 - c, x))
SPREAD = [joint(spread_move(p)) for p in range(4)]
COLLECT = [joint(collect_move(r)) for r in range(2)]
RING_X = joint(lambda y, c, x: (y, c, (x + 1 + 2 * c) % 4))
RING_Y = joint(lambda y, c, x: ((y + 1 + 2 * c) % 4, c, x))


def move(value, pairs):
    return lax.ppermute(value, AXES, pairs)


def split(a):
    high = a.astype(jnp.bfloat16)
    return high, (a - high.astype(F32)).astype(jnp.bfloat16)


def dot(a, b):
    return jnp.dot(a, b, preferred_element_type=F32)


def mm3(a, b):
    return dot(a[0], b[0]) + (dot(a[0], b[1]) + dot(a[1], b[0]))


def rows_times(row8, matrix):
    column = jnp.transpose(row8)[:, 0:1]
    product = (matrix * column).reshape(matrix.shape[0] // 8, 8, matrix.shape[1])
    total = jnp.sum(jnp.sum(product, axis=0), axis=0, keepdims=True)
    return jnp.broadcast_to(total, (8, matrix.shape[1]))


def block(i):
    return pl.ds(pl.multiple_of(i * B, B), B)


def place():
    tm = lax.axis_index("tm")
    return lax.axis_index("state"), lax.rem(tm // 2, 4), tm // 8, lax.rem(tm, 2)


def next_block(x, skip):
    one = lax.rem(x + 1, 4)
    return jnp.where(one == skip, lax.rem(x + 2, 4), one)


def pack_kernel(
    p_ref, r_ref, t_ref, m_ref, q_ref, i_ref, pay0, pay1, pay2, pay3, local_ref, other_ref, means, ids, sems
):
    x, _, _, c = place()
    copies = []

    def start(source, target):
        copy = pltpu.make_async_copy(source, target, sems.at[len(copies)])
        copy.start()
        copies.append(copy)

    start(m_ref, means.at[0])
    start(q_ref, means.at[1])
    start(i_ref, ids)
    for p, pay in enumerate((pay0, pay1, pay2, pay3)):
        j = lax.rem(x + p, 4)
        after = next_block(x, 2 * lax.rem(j // 2, 2) + c)
        for row, ref in ((0, p_ref), (B, r_ref)):
            start(ref.at[j, :, block(x)], pay.at[row : row + B, 0:B])
            start(ref.at[j, :, block(after)], pay.at[row : row + B, B : 2 * B])
        start(t_ref.at[j, 0], pay.at[256:320, 0:B])
        start(t_ref.at[j, 1], pay.at[256:320, B : 2 * B])
    mine = 2 * (x // 2) + c
    theirs = 2 * (x // 2) + 1 - c
    for row, ref in ((0, p_ref), (B, r_ref)):
        start(ref.at[mine], local_ref.at[row : row + B])
        start(ref.at[theirs], other_ref.at[row : row + B])
    for copy in copies[:3]:
        copy.wait()
    lane = lax.broadcasted_iota(jnp.int32, (2, 8), 1)
    low = lax.broadcasted_iota(jnp.int32, (1, B), 1) < 64
    for p, pay in enumerate((pay0, pay1, pay2, pay3)):
        j = lax.rem(x + p, 4)
        pay[320:321, 0:B] = means[0, pl.ds(j, 1), :]
        pay[320:321, B : 2 * B] = means[1, pl.ds(j, 1), :]
        for half in range(2):
            pair = jnp.sum(
                jnp.where(lane == 2 * x + half, ids[j].astype(F32), 0.0), axis=1, keepdims=True
            )
            first = jnp.broadcast_to(pair[0:1], (1, B))
            second = jnp.broadcast_to(pair[1:2], (1, B))
            pay[321:322, half * B : (half + 1) * B] = jnp.where(low, first, second)
            pay[322:323, half * B : (half + 1) * B] = jnp.where(low, second, first)
    for copy in copies[3:]:
        copy.wait()


def step_kernel(pay0, pay1, pay2, pay3, local_ref, other_ref, out_ref, pf, rf, inc, vec):
    x, y, z, c = place()
    j = 2 * (x // 2) + c
    same = lax.rem(x, 2) == c
    low = lax.broadcasted_iota(jnp.int32, (64, B), 1) < 64
    for p, pay in enumerate((pay0, pay1, pay2, pay3)):
        source = lax.rem(j - p + 4, 4)
        after = next_block(source, x)
        for row, full in ((0, pf), (B, rf)):
            full[block(source), block(source)] = pay[row : row + B, 0:B]
            beside = pay[row : row + B, B : 2 * B]
            full[block(source), block(after)] = beside
            full[block(after), block(source)] = jnp.transpose(beside)
        for half in range(2):
            r = 2 * source + half
            lanes = slice(half * B, (half + 1) * B)
            tiles = pay[256:320, lanes]
            turned = jnp.concatenate([tiles[:, 64:], tiles[:, :64]], axis=1)
            straight_to = jnp.broadcast_to(pay[321:322, lanes], (64, B))
            turned_to = jnp.broadcast_to(pay[322:323, lanes], (64, B))
            for g in range(4):
                here = jnp.where(low, 2.0 * g, 2.0 * g + 1.0)
                value = jnp.where(
                    straight_to == here, tiles, jnp.where(turned_to == here, turned, 0.0)
                )
                inc[pl.ds(pl.multiple_of(r * 64, 64), 64), g * B : (g + 1) * B] = value
        vec[0:8, block(source)] = jnp.broadcast_to(pay[320:321, 0:B], (8, B))
        vec[8:16, block(source)] = jnp.broadcast_to(pay[320:321, B : 2 * B], (8, B))
    for row, full in ((0, pf), (B, rf)):
        full[block(x), :] = jnp.where(
            same, local_ref[row : row + B, :], other_ref[row : row + B, :]
        )
        for d in (1, 2, 3):
            v = lax.rem(x + d, 4)
            full[block(v), block(x)] = jnp.transpose(full[block(x), block(v)])
    mixed = pf[...] + mm3(split(inc[...]), split(pf[...]))
    mixed = split(mixed)
    precision = split(rf[...])
    lead = split(mm3(split(vec[8:16, :]), precision))
    last = (z == NZ - 1) & (y == NY - 1) & (x == NX - 1) & (c == NC - 1)
    gain = mm3(precision, mixed)
    out_ref[0:W, :] = jnp.where(last, 0.0, gain)
    out_ref[W:FULL, :] = vec[0:8, :] - jnp.where(last, 0.0, mm3(lead, mixed))


def halves(ref, c):
    n = pl.multiple_of(c * HALF, HALF)
    m = pl.multiple_of((1 - c) * HALF, HALF)
    return ref[pl.ds(n, HALF), :], ref[pl.ds(m, HALF), :]


def pair_kernel(own_ref, other_ref, first_ref, second_ref):
    _, _, _, c = place()

    def compose(early, late):
        rows = jnp.concatenate([*halves(early, c), early[W:FULL, :]], axis=0)
        value = mm3(split(rows), split(late[0:W, :]))
        tail = value[W:] + late[W:FULL, :]
        for n, ref in enumerate((first_ref, second_ref)):
            ref[0:HALF, :] = value[n * HALF : (n + 1) * HALF]
            ref[HALF:PAN, :] = tail

    @pl.when(c == 0)
    def _():
        compose(other_ref, own_ref)

    @pl.when(c == 1)
    def _():
        compose(own_ref, other_ref)


def fetch(panels, held, sems, index, c, turned):
    forth, back, far = index + 3 - 2 * c, index + 1 + 2 * c, index + 2
    homes = ((index, c), (index, 1 - c), (forth, c), (forth, 1 - c), (back, 1 - c), (back, c), (far, c), (far, 1 - c))
    copies = []
    for n, (ref, (source, half)) in enumerate(zip(panels, homes)):
        slot = lax.rem(source, 4)
        if turned:
            slot = 2 * lax.rem(slot, 2) + slot // 2
        copy = pltpu.make_async_copy(ref, held.at[slot, half], sems.at[n])
        copy.start()
        copies.append(copy)
    return copies


def chain_kernel(along, whole, *refs):
    panels, held, prefix, outs, sems = refs[:8], refs[8], refs[9], refs[10:-1], refs[-1]
    x, y, _, c = place()
    for copy in fetch(panels, held, sems, x if along == "x" else y, c, along == "x"):
        copy.wait()
    tail = held[3, 0, HALF:PAN, :]
    begin = 0 if whole else c
    rows = jnp.concatenate([held[3, begin, 0:HALF, :], held[3, 1 - begin, 0:HALF, :], tail], axis=0)

    if whole:
        prefix[2] = rows
    for t in (2, 1, 0):
        left = split(rows)
        top = split(held[t, 0, 0:HALF, :])
        bottom = split(held[t, 1, 0:HALF, :])
        value = mm3((left[0][:, :HALF], left[1][:, :HALF]), top) + mm3(
            (left[0][:, HALF:], left[1][:, HALF:]), bottom
        )
        rows = jnp.concatenate([value[0:W], value[W:] + held[t, 0, HALF:PAN, :]], axis=0)
        if whole and t > 0:
            prefix[t - 1] = rows
        if not whole and t == 2:
            prefix[pl.ds(pl.multiple_of(c * HALF, HALF), HALF), :] = rows[0:HALF]
            prefix[pl.ds(pl.multiple_of((1 - c) * HALF, HALF), HALF), :] = rows[HALF:W]
            prefix[W:FULL, :] = rows[W:FULL]
    if whole:
        outs[0][...] = rows
    else:
        for n in range(2):
            outs[n][0:HALF, :] = rows[n * HALF : (n + 1) * HALF]
            outs[n][HALF:PAN, :] = rows[W:FULL]


def plane_kernel(map_ref, carried_ref, came_ref, carried_out, out_ref):
    carried = carried_ref[...] + came_ref[...]
    carried_out[...] = carried
    out_ref[...] = rows_times(carried, map_ref[0:W, :]) + map_ref[W:FULL, :]


def columns_kernel(own_ref, other_ref, after_ref, send0, send1):
    x, _, _, c = place()

    def cut(odd):
        for r, send in enumerate((send0, send1)):
            send[...] = odd[:, block(2 * c + lax.rem(x // 2 + r, 2))]

    @pl.when(c == 0)
    def _():
        cut(other_ref)

    @pl.when(c == 1)
    def _():
        cut(own_ref)


def down_kernel(carried_ref, came_ref, cut0_ref, cut1_ref, rows_ref, pairs_ref, held_x, out_ref):
    x, y, _, c = place()

    def apply(row8, ref):
        return rows_times(row8, ref[0:W, :]) + ref[W:FULL, :]

    def pair(row8, t, lanes):
        matrix = jnp.concatenate([held_x[t, 0, 0:HALF, lanes], held_x[t, 1, 0:HALF, lanes]], axis=0)
        return rows_times(row8, matrix) + held_x[t, 0, HALF:PAN, lanes]

    def odd(row8, parity):
        cut = jnp.where(lax.rem(x, 2) == parity, cut0_ref[...], cut1_ref[...])
        return (rows_times(row8, cut[0:W]) + cut[W:FULL])[0:1]

    late = carried_ref[...] + came_ref[...]
    late = jnp.where(y == 3, late, apply(late, rows_ref.at[jnp.minimum(y, 2)]))
    late = jnp.where(c == 1, late, apply(late, pairs_ref))
    early = pair(late, 2 * c + 1, slice(None))
    out_ref[3:4, :] = odd(late, 1)
    out_ref[2:3, :] = pair(late, 2 * c + 1, block(x))[0:1]
    out_ref[1:2, :] = odd(early, 0)
    out_ref[0:1, :] = pair(early, 2 * c, block(x))[0:1]


def shape(*dims):
    return jax.ShapeDtypeStruct(dims, F32)


PARAMS = pltpu.CompilerParams(vmem_limit_bytes=VMEM_LIMIT)
IN_VMEM = pl.BlockSpec(memory_space=pltpu.VMEM)
IN_HBM = pl.BlockSpec(memory_space=pltpu.HBM)
ANYWHERE = pl.BlockSpec(memory_space=pl.ANY)


def gather_panels(first, second, ring, beside=None):
    one, two = move(first, ring), move(second, ring)
    far = move(one, ring)
    if beside is not None:
        two, *beside = lax.optimization_barrier((two, *beside))
    panels = first, second, one, two, move(one, SWAP), move(two, SWAP), far, move(far, SWAP)
    return panels, beside


def chain(along, whole, panels):
    def kernel(*refs):
        chain_kernel(along, whole, *refs)

    return pl.pallas_call(
        kernel,
        out_shape=[shape(4, 2, PAN, W), shape(3, FULL, W) if whole else shape(FULL, W)]
        + ([shape(FULL, W)] if whole else [shape(PAN, W)] * 2),
        in_specs=[ANYWHERE] * 8,
        out_specs=[IN_VMEM] * (3 if whole else 4),
        scratch_shapes=[pltpu.SemaphoreType.DMA((8,))],
        compiler_params=PARAMS,
        name="chain_" + along,
    )(*panels)


def in_hbm(value):
    return pltpu.with_memory_space_constraint(value, pltpu.HBM)


def on_device(spread, inverse, tiles, ids, mean, prior):
    *pays, local, other = pl.pallas_call(
        pack_kernel,
        out_shape=[shape(328, HALF)] * 4 + [shape(2 * B, W)] * 2,
        in_specs=[IN_HBM] * 6,
        out_specs=[IN_VMEM] * 6,
        scratch_shapes=[
            pltpu.VMEM((2, 4, B), F32),
            pltpu.VMEM((4, 2, 8), jnp.int32),
            pltpu.SemaphoreType.DMA((31,)),
        ],
        compiler_params=PARAMS,
        name="pack",
    )(*(in_hbm(a) for a in (spread, inverse, tiles, mean, prior, jnp.swapaxes(ids, 1, 2))))
    got = [move(pay, SPREAD[p]) for p, pay in enumerate(pays)]
    other = move(other, SWAP)
    step = pl.pallas_call(
        step_kernel,
        out_shape=shape(FULL, W),
        in_specs=[IN_VMEM] * 6,
        out_specs=IN_VMEM,
        scratch_shapes=[pltpu.VMEM((W, W), F32)] * 3 + [pltpu.VMEM((16, W), F32)],
        compiler_params=PARAMS,
        name="step",
    )(*got, local, other)
    twin = move(step, SWAP)
    pair = pl.pallas_call(
        pair_kernel,
        out_shape=[shape(PAN, W)] * 2,
        in_specs=[IN_VMEM] * 2,
        out_specs=[IN_VMEM] * 2,
        compiler_params=PARAMS,
        name="pair",
    )(step, twin)
    held_x, pairs_map, *row_map = chain("x", False, gather_panels(*pair, RING_X)[0])
    cuts = pl.pallas_call(
        columns_kernel,
        out_shape=[shape(FULL, B)] * 2,
        in_specs=[IN_VMEM] * 2 + [ANYWHERE],
        out_specs=[IN_VMEM] * 2,
        compiler_params=PARAMS,
        name="columns",
    )(step, twin, row_map[0])
    cuts = [move(cut, COLLECT[r]) for r, cut in enumerate(cuts)]
    panels_y, cuts = gather_panels(*row_map, RING_Y, cuts)
    _, rows_map, plane_map = chain("y", True, panels_y)
    carried = jnp.zeros((8, W), F32)
    came = jnp.zeros((8, W), F32)
    for i in range(NZ - 1):
        carried, out = pl.pallas_call(
            plane_kernel,
            out_shape=[shape(8, W)] * 2,
            in_specs=[IN_VMEM] * 3,
            out_specs=[IN_VMEM] * 2,
            compiler_params=PARAMS,
            name="plane",
        )(plane_map, carried, came)
        came = lax.ppermute(out, "tm", [(t, t - 8) for t in range(64) if t // 8 == 7 - i and t % 2])
    carried = carried + came
    came = lax.ppermute(carried, "tm", [(t, t - 1) for t in range(64) if t % 2])
    return pl.pallas_call(
        down_kernel,
        out_shape=shape(4, B),
        in_specs=[IN_VMEM] * 7,
        out_specs=IN_VMEM,
        compiler_params=PARAMS,
        name="down",
    )(carried, came, *cuts, rows_map, pairs_map, held_x)


def solution(mesh):
    return jax.shard_map(
        on_device,
        mesh=mesh,
        in_specs=(
            P("tm", "state", None),
            P("tm", "state", None),
            P("tm", "state", None, None),
            P("tm", None, None),
            P("tm", "state"),
            P("tm", "state"),
        ),
        out_specs=P("tm", "state"),
        check_vma=False,
    )
```

```python
import jax
import jax.numpy as jnp
from jax import lax
from jax.experimental import pallas as pl
from jax.experimental.pallas import tpu as pltpu
from jax.sharding import PartitionSpec as P

NZ, NY, NC, NX = 8, 4, 2, 4
W = 512
B = 128
HALF = 256
PAN = HALF + 8
FULL = W + 8
AXES = ("tm", "state")
F32 = jnp.float32
VMEM_LIMIT = 24 * 1024 * 1024


def turn(x):
    return 2 * (x % 2) + x // 2


def joint(move):
    pairs = []
    for z in range(NZ):
        for y in range(NY):
            for c in range(NC):
                for x in range(NX):
                    y2, c2, x2 = move(y, c, x)
                    source = ((z * NY + y) * NC + c) * NX + x
                    pairs.append((source, ((z * NY + y2) * NC + c2) * NX + x2))
    return pairs


def spread_move(p):
    def move(y, c, x):
        q = (x + p) % 4
        return y, q % 2, turn(2 * c + q // 2)

    return move


def collect_move(r):
    def move(y, c, x):
        return y, x % 2, 2 * c + (x // 2 + r) % 2

    return move


SWAP = joint(lambda y, c, x: (y, 1 - c, x))
SPREAD = [joint(spread_move(p)) for p in range(4)]
COLLECT = [joint(collect_move(r)) for r in range(2)]
RING_X = joint(lambda y, c, x: (y, c, (x + 1 + 2 * c) % 4))
RING_Y = joint(lambda y, c, x: ((y + 1 + 2 * c) % 4, c, x))


def move(value, pairs):
    return lax.ppermute(value, AXES, pairs)


def split(a):
    high = a.astype(jnp.bfloat16)
    return high, (a - high.astype(F32)).astype(jnp.bfloat16)


def dot(a, b):
    return jnp.dot(a, b, preferred_element_type=F32)


def mm3(a, b):
    return dot(a[0], b[0]) + (dot(a[0], b[1]) + dot(a[1], b[0]))


def rows_times(row8, matrix):
    column = jnp.transpose(row8)[:, 0:1]
    product = (matrix * column).reshape(matrix.shape[0] // 8, 8, matrix.shape[1])
    total = jnp.sum(jnp.sum(product, axis=0), axis=0, keepdims=True)
    return jnp.broadcast_to(total, (8, matrix.shape[1]))


def block(i):
    return pl.ds(pl.multiple_of(i * B, B), B)


def place():
    tm = lax.axis_index("tm")
    return lax.axis_index("state"), lax.rem(tm // 2, 4), tm // 8, lax.rem(tm, 2)


def next_block(x, skip):
    one = lax.rem(x + 1, 4)
    return jnp.where(one == skip, lax.rem(x + 2, 4), one)


def pack_kernel(
    p_ref, r_ref, t_ref, m_ref, q_ref, i_ref, pay0, pay1, pay2, pay3, local_ref, other_ref, means, ids, sems
):
    x, _, _, c = place()
    copies = []

    def start(source, target):
        copy = pltpu.make_async_copy(source, target, sems.at[len(copies)])
        copy.start()
        copies.append(copy)

    start(m_ref, means.at[0])
    start(q_ref, means.at[1])
    start(i_ref, ids)
    for p, pay in enumerate((pay0, pay1, pay2, pay3)):
        j = lax.rem(x + p, 4)
        after = next_block(x, 2 * lax.rem(j // 2, 2) + c)
        for row, ref in ((0, p_ref), (B, r_ref)):
            start(ref.at[j, :, block(x)], pay.at[row : row + B, 0:B])
            start(ref.at[j, :, block(after)], pay.at[row : row + B, B : 2 * B])
        start(t_ref.at[j, 0], pay.at[256:320, 0:B])
        start(t_ref.at[j, 1], pay.at[256:320, B : 2 * B])
    mine = 2 * (x // 2) + c
    theirs = 2 * (x // 2) + 1 - c
    for row, ref in ((0, p_ref), (B, r_ref)):
        start(ref.at[mine], local_ref.at[row : row + B])
        start(ref.at[theirs], other_ref.at[row : row + B])
    for copy in copies[:3]:
        copy.wait()
    lane = lax.broadcasted_iota(jnp.int32, (2, 8), 1)
    low = lax.broadcasted_iota(jnp.int32, (1, B), 1) < 64
    for p, pay in enumerate((pay0, pay1, pay2, pay3)):
        j = lax.rem(x + p, 4)
        pay[320:321, 0:B] = means[0, pl.ds(j, 1), :]
        pay[320:321, B : 2 * B] = means[1, pl.ds(j, 1), :]
        for half in range(2):
            pair = jnp.sum(
                jnp.where(lane == 2 * x + half, ids[j].astype(F32), 0.0), axis=1, keepdims=True
            )
            first = jnp.broadcast_to(pair[0:1], (1, B))
            second = jnp.broadcast_to(pair[1:2], (1, B))
            pay[321:322, half * B : (half + 1) * B] = jnp.where(low, first, second)
            pay[322:323, half * B : (half + 1) * B] = jnp.where(low, second, first)
    for copy in copies[3:]:
        copy.wait()


def step_kernel(pay0, pay1, pay2, pay3, local_ref, other_ref, out_ref, pf, rf, inc, vec):
    x, y, z, c = place()
    j = 2 * (x // 2) + c
    same = lax.rem(x, 2) == c
    low = lax.broadcasted_iota(jnp.int32, (64, B), 1) < 64
    for p, pay in enumerate((pay0, pay1, pay2, pay3)):
        source = lax.rem(j - p + 4, 4)
        after = next_block(source, x)
        for row, full in ((0, pf), (B, rf)):
            full[block(source), block(source)] = pay[row : row + B, 0:B]
            beside = pay[row : row + B, B : 2 * B]
            full[block(source), block(after)] = beside
            full[block(after), block(source)] = jnp.transpose(beside)
        for half in range(2):
            r = 2 * source + half
            lanes = slice(half * B, (half + 1) * B)
            tiles = pay[256:320, lanes]
            turned = jnp.concatenate([tiles[:, 64:], tiles[:, :64]], axis=1)
            straight_to = jnp.broadcast_to(pay[321:322, lanes], (64, B))
            turned_to = jnp.broadcast_to(pay[322:323, lanes], (64, B))
            for g in range(4):
                here = jnp.where(low, 2.0 * g, 2.0 * g + 1.0)
                value = jnp.where(
                    straight_to == here, tiles, jnp.where(turned_to == here, turned, 0.0)
                )
                inc[pl.ds(pl.multiple_of(r * 64, 64), 64), g * B : (g + 1) * B] = value
        vec[0:8, block(source)] = jnp.broadcast_to(pay[320:321, 0:B], (8, B))
        vec[8:16, block(source)] = jnp.broadcast_to(pay[320:321, B : 2 * B], (8, B))
    for row, full in ((0, pf), (B, rf)):
        full[block(x), :] = jnp.where(
            same, local_ref[row : row + B, :], other_ref[row : row + B, :]
        )
        for d in (1, 2, 3):
            v = lax.rem(x + d, 4)
            full[block(v), block(x)] = jnp.transpose(full[block(x), block(v)])
    mixed = pf[...] + mm3(split(inc[...]), split(pf[...]))
    mixed = split(mixed)
    precision = split(rf[...])
    lead = split(mm3(split(vec[8:16, :]), precision))
    last = (z == NZ - 1) & (y == NY - 1) & (x == NX - 1) & (c == NC - 1)
    gain = mm3(precision, mixed)
    out_ref[0:W, :] = jnp.where(last, 0.0, gain)
    out_ref[W:FULL, :] = vec[0:8, :] - jnp.where(last, 0.0, mm3(lead, mixed))


def halves(ref, c):
    n = pl.multiple_of(c * HALF, HALF)
    m = pl.multiple_of((1 - c) * HALF, HALF)
    return ref[pl.ds(n, HALF), :], ref[pl.ds(m, HALF), :]


def pair_kernel(own_ref, other_ref, first_ref, second_ref):
    _, _, _, c = place()

    def compose(early, late):
        rows = jnp.concatenate([*halves(early, c), early[W:FULL, :]], axis=0)
        value = mm3(split(rows), split(late[0:W, :]))
        tail = value[W:] + late[W:FULL, :]
        for n, ref in enumerate((first_ref, second_ref)):
            ref[0:HALF, :] = value[n * HALF : (n + 1) * HALF]
            ref[HALF:PAN, :] = tail

    @pl.when(c == 0)
    def _():
        compose(other_ref, own_ref)

    @pl.when(c == 1)
    def _():
        compose(own_ref, other_ref)


def fetch(panels, held, sems, index, c, turned):
    forth, back, far = index + 3 - 2 * c, index + 1 + 2 * c, index + 2
    homes = ((index, c), (index, 1 - c), (forth, c), (forth, 1 - c), (back, 1 - c), (back, c), (far, c), (far, 1 - c))
    copies = []
    for n, (ref, (source, half)) in enumerate(zip(panels, homes)):
        slot = lax.rem(source, 4)
        if turned:
            slot = 2 * lax.rem(slot, 2) + slot // 2
        copy = pltpu.make_async_copy(ref, held.at[slot, half], sems.at[n])
        copy.start()
        copies.append(copy)
    return copies


def lead_kernel(*refs):
    panels, held, lead_ref, sems = refs[:8], refs[8], refs[9], refs[10]
    _, y, _, c = place()
    for copy in fetch(panels, held, sems, y, c, False):
        copy.wait()
    row8 = held[3, 0, HALF:PAN, :]
    for t in (2, 1, 0):
        row8 = (
            rows_times(row8[:, 0:HALF], held[t, 0, 0:HALF, :])
            + rows_times(row8[:, HALF:W], held[t, 1, 0:HALF, :])
            + held[t, 0, HALF:PAN, :]
        )
    lead_ref[...] = row8


def chain_kernel(along, whole, *refs):
    if whole:
        held, prefix, outs = refs[0], refs[1], refs[2:]
    else:
        panels, held, prefix, outs, sems = refs[:8], refs[8], refs[9], refs[10:-1], refs[-1]
    x, y, _, c = place()
    if not whole:
        for copy in fetch(panels, held, sems, x, c, True):
            copy.wait()
    tail = held[3, 0, HALF:PAN, :]
    begin = 0 if whole else c
    rows = jnp.concatenate([held[3, begin, 0:HALF, :], held[3, 1 - begin, 0:HALF, :], tail], axis=0)

    if whole:
        prefix[2] = rows
    for t in (2, 1, 0):
        left = split(rows)
        top = split(held[t, 0, 0:HALF, :])
        bottom = split(held[t, 1, 0:HALF, :])
        value = mm3((left[0][:, :HALF], left[1][:, :HALF]), top) + mm3(
            (left[0][:, HALF:], left[1][:, HALF:]), bottom
        )
        rows = jnp.concatenate([value[0:W], value[W:] + held[t, 0, HALF:PAN, :]], axis=0)
        if whole and t > 0:
            prefix[t - 1] = rows
        if not whole and t == 2:
            prefix[pl.ds(pl.multiple_of(c * HALF, HALF), HALF), :] = rows[0:HALF]
            prefix[pl.ds(pl.multiple_of((1 - c) * HALF, HALF), HALF), :] = rows[HALF:W]
            prefix[W:FULL, :] = rows[W:FULL]
    if whole:
        outs[0][...] = rows
    else:
        for n in range(2):
            outs[n][0:HALF, :] = rows[n * HALF : (n + 1) * HALF]
            outs[n][HALF:PAN, :] = rows[W:FULL]


def plane_kernel(map_ref, carried_ref, came_ref, carried_out, out_ref):
    carried = carried_ref[...] + came_ref[...]
    carried_out[...] = carried
    out_ref[...] = rows_times(carried, map_ref[0:W, :]) + map_ref[W:FULL, :]


def columns_kernel(own_ref, other_ref, after_ref, send0, send1):
    x, _, _, c = place()

    def cut(odd):
        for r, send in enumerate((send0, send1)):
            send[...] = odd[:, block(2 * c + lax.rem(x // 2 + r, 2))]

    @pl.when(c == 0)
    def _():
        cut(other_ref)

    @pl.when(c == 1)
    def _():
        cut(own_ref)


def down_kernel(carried_ref, came_ref, cut0_ref, cut1_ref, rows_ref, pairs_ref, held_x, out_ref):
    x, y, _, c = place()

    def apply(row8, ref):
        return rows_times(row8, ref[0:W, :]) + ref[W:FULL, :]

    def pair(row8, t, lanes):
        matrix = jnp.concatenate([held_x[t, 0, 0:HALF, lanes], held_x[t, 1, 0:HALF, lanes]], axis=0)
        return rows_times(row8, matrix) + held_x[t, 0, HALF:PAN, lanes]

    def odd(row8, parity):
        cut = jnp.where(lax.rem(x, 2) == parity, cut0_ref[...], cut1_ref[...])
        return (rows_times(row8, cut[0:W]) + cut[W:FULL])[0:1]

    late = carried_ref[...] + came_ref[...]
    late = jnp.where(y == 3, late, apply(late, rows_ref.at[jnp.minimum(y, 2)]))
    late = jnp.where(c == 1, late, apply(late, pairs_ref))
    early = pair(late, 2 * c + 1, slice(None))
    out_ref[3:4, :] = odd(late, 1)
    out_ref[2:3, :] = pair(late, 2 * c + 1, block(x))[0:1]
    out_ref[1:2, :] = odd(early, 0)
    out_ref[0:1, :] = pair(early, 2 * c, block(x))[0:1]


def shape(*dims):
    return jax.ShapeDtypeStruct(dims, F32)


PARAMS = pltpu.CompilerParams(vmem_limit_bytes=VMEM_LIMIT)
IN_VMEM = pl.BlockSpec(memory_space=pltpu.VMEM)
IN_HBM = pl.BlockSpec(memory_space=pltpu.HBM)
ANYWHERE = pl.BlockSpec(memory_space=pl.ANY)


def gather_panels(first, second, ring, beside=None):
    one, two = move(first, ring), move(second, ring)
    far = move(one, ring)
    if beside is not None:
        two, *beside = lax.optimization_barrier((two, *beside))
    panels = first, second, one, two, move(one, SWAP), move(two, SWAP), far, move(far, SWAP)
    return panels, beside


def lead(panels):
    return pl.pallas_call(
        lead_kernel,
        out_shape=[shape(4, 2, PAN, W), shape(8, W)],
        in_specs=[ANYWHERE] * 8,
        out_specs=[IN_VMEM] * 2,
        scratch_shapes=[pltpu.SemaphoreType.DMA((8,))],
        compiler_params=PARAMS,
        name="lead",
    )(*panels)


def chain(along, whole, operands):
    def kernel(*refs):
        chain_kernel(along, whole, *refs)

    outs = [shape(4, 2, PAN, W), shape(FULL, W)] + [shape(PAN, W)] * 2
    if whole:
        outs = [shape(3, FULL, W), shape(FULL, W)]
    return pl.pallas_call(
        kernel,
        out_shape=outs,
        in_specs=[IN_VMEM] if whole else [ANYWHERE] * 8,
        out_specs=[IN_VMEM] * len(outs),
        scratch_shapes=[] if whole else [pltpu.SemaphoreType.DMA((8,))],
        compiler_params=PARAMS,
        name="chain_" + along,
    )(*operands)


def in_hbm(value):
    return pltpu.with_memory_space_constraint(value, pltpu.HBM)


def on_device(spread, inverse, tiles, ids, mean, prior):
    *pays, local, other = pl.pallas_call(
        pack_kernel,
        out_shape=[shape(328, HALF)] * 4 + [shape(2 * B, W)] * 2,
        in_specs=[IN_HBM] * 6,
        out_specs=[IN_VMEM] * 6,
        scratch_shapes=[
            pltpu.VMEM((2, 4, B), F32),
            pltpu.VMEM((4, 2, 8), jnp.int32),
            pltpu.SemaphoreType.DMA((31,)),
        ],
        compiler_params=PARAMS,
        name="pack",
    )(*(in_hbm(a) for a in (spread, inverse, tiles, mean, prior, jnp.swapaxes(ids, 1, 2))))
    got = [move(pay, SPREAD[p]) for p, pay in enumerate(pays)]
    other = move(other, SWAP)
    step = pl.pallas_call(
        step_kernel,
        out_shape=shape(FULL, W),
        in_specs=[IN_VMEM] * 6,
        out_specs=IN_VMEM,
        scratch_shapes=[pltpu.VMEM((W, W), F32)] * 3 + [pltpu.VMEM((16, W), F32)],
        compiler_params=PARAMS,
        name="step",
    )(*got, local, other)
    twin = move(step, SWAP)
    pair = pl.pallas_call(
        pair_kernel,
        out_shape=[shape(PAN, W)] * 2,
        in_specs=[IN_VMEM] * 2,
        out_specs=[IN_VMEM] * 2,
        compiler_params=PARAMS,
        name="pair",
    )(step, twin)
    held_x, pairs_map, *row_map = chain("x", False, gather_panels(*pair, RING_X)[0])
    cuts = pl.pallas_call(
        columns_kernel,
        out_shape=[shape(FULL, B)] * 2,
        in_specs=[IN_VMEM] * 2 + [ANYWHERE],
        out_specs=[IN_VMEM] * 2,
        compiler_params=PARAMS,
        name="columns",
    )(step, twin, row_map[0])
    cuts = [move(cut, COLLECT[r]) for r, cut in enumerate(cuts)]
    panels_y, cuts = gather_panels(*row_map, RING_Y, cuts)
    held_y, out = lead(panels_y)
    rows_map, plane_map = chain("y", True, [held_y])
    carried = jnp.zeros((8, W), F32)
    came = jnp.zeros((8, W), F32)
    for i in range(NZ - 1):
        if i > 0:
            carried, out = pl.pallas_call(
                plane_kernel,
                out_shape=[shape(8, W)] * 2,
                in_specs=[IN_VMEM] * 3,
                out_specs=[IN_VMEM] * 2,
                compiler_params=PARAMS,
                name="plane",
            )(plane_map, carried, came)
        came = lax.ppermute(out, "tm", [(t, t - 8) for t in range(64) if t // 8 == 7 - i and t % 2])
    carried = carried + came
    came = lax.ppermute(carried, "tm", [(t, t - 1) for t in range(64) if t % 2])
    return pl.pallas_call(
        down_kernel,
        out_shape=shape(4, B),
        in_specs=[IN_VMEM] * 7,
        out_specs=IN_VMEM,
        compiler_params=PARAMS,
        name="down",
    )(carried, came, *cuts, rows_map, pairs_map, held_x)


def solution(mesh):
    return jax.shard_map(
        on_device,
        mesh=mesh,
        in_specs=(
            P("tm", "state", None),
            P("tm", "state", None),
            P("tm", "state", None, None),
            P("tm", None, None),
            P("tm", "state"),
            P("tm", "state"),
        ),
        out_specs=P("tm", "state"),
        check_vma=False,
    )
```

```python
import jax
import jax.numpy as jnp
from jax import lax
from jax.experimental import pallas as pl
from jax.experimental.pallas import tpu as pltpu
from jax.sharding import PartitionSpec as P

NZ, NY, NC, NX = 8, 4, 2, 4
W = 512
B = 128
HALF = 256
PAN = HALF + 8
FULL = W + 8
AXES = ("tm", "state")
F32 = jnp.float32
VMEM_LIMIT = 24 * 1024 * 1024


def turn(x):
    return 2 * (x % 2) + x // 2


def joint(move):
    pairs = []
    for z in range(NZ):
        for y in range(NY):
            for c in range(NC):
                for x in range(NX):
                    y2, c2, x2 = move(y, c, x)
                    source = ((z * NY + y) * NC + c) * NX + x
                    pairs.append((source, ((z * NY + y2) * NC + c2) * NX + x2))
    return pairs


def spread_move(p):
    def move(y, c, x):
        q = (x + p) % 4
        return y, q % 2, turn(2 * c + q // 2)

    return move


def collect_move(r):
    def move(y, c, x):
        return y, x % 2, 2 * c + (x // 2 + r) % 2

    return move


SWAP = joint(lambda y, c, x: (y, 1 - c, x))
SPREAD = [joint(spread_move(p)) for p in range(4)]
COLLECT = [joint(collect_move(r)) for r in range(2)]
RING_X = joint(lambda y, c, x: (y, c, (x + 1 + 2 * c) % 4))
RING_Y = joint(lambda y, c, x: ((y + 1 + 2 * c) % 4, c, x))


def move(value, pairs):
    return lax.ppermute(value, AXES, pairs)


def split(a):
    high = a.astype(jnp.bfloat16)
    return high, (a - high.astype(F32)).astype(jnp.bfloat16)


def dot(a, b):
    return jnp.dot(a, b, preferred_element_type=F32)


def mm3(a, b):
    return dot(a[0], b[0]) + (dot(a[0], b[1]) + dot(a[1], b[0]))


def rows_times(row8, matrix):
    column = jnp.transpose(row8)[:, 0:1]
    product = (matrix * column).reshape(matrix.shape[0] // 8, 8, matrix.shape[1])
    total = jnp.sum(jnp.sum(product, axis=0), axis=0, keepdims=True)
    return jnp.broadcast_to(total, (8, matrix.shape[1]))


def block(i):
    return pl.ds(pl.multiple_of(i * B, B), B)


def place():
    tm = lax.axis_index("tm")
    return lax.axis_index("state"), lax.rem(tm // 2, 4), tm // 8, lax.rem(tm, 2)


def next_block(x, skip):
    one = lax.rem(x + 1, 4)
    return jnp.where(one == skip, lax.rem(x + 2, 4), one)


def pack_kernel(
    p_ref, r_ref, t_ref, m_ref, q_ref, i_ref, pay0, pay1, pay2, pay3, local_ref, other_ref, means, ids, sems
):
    x, _, _, c = place()
    copies = []

    def start(source, target):
        copy = pltpu.make_async_copy(source, target, sems.at[len(copies)])
        copy.start()
        copies.append(copy)

    start(m_ref, means.at[0])
    start(q_ref, means.at[1])
    start(i_ref, ids)
    for p, pay in enumerate((pay0, pay1, pay2, pay3)):
        j = lax.rem(x + p, 4)
        after = next_block(x, 2 * lax.rem(j // 2, 2) + c)
        for row, ref in ((0, p_ref), (B, r_ref)):
            start(ref.at[j, :, block(x)], pay.at[row : row + B, 0:B])
            start(ref.at[j, :, block(after)], pay.at[row : row + B, B : 2 * B])
        start(t_ref.at[j, 0], pay.at[256:320, 0:B])
        start(t_ref.at[j, 1], pay.at[256:320, B : 2 * B])
    mine = 2 * (x // 2) + c
    theirs = 2 * (x // 2) + 1 - c
    for row, ref in ((0, p_ref), (B, r_ref)):
        start(ref.at[mine], local_ref.at[row : row + B])
        start(ref.at[theirs], other_ref.at[row : row + B])
    for copy in copies[:3]:
        copy.wait()
    lane = lax.broadcasted_iota(jnp.int32, (2, 8), 1)
    low = lax.broadcasted_iota(jnp.int32, (1, B), 1) < 64
    for p, pay in enumerate((pay0, pay1, pay2, pay3)):
        j = lax.rem(x + p, 4)
        pay[320:321, 0:B] = means[0, pl.ds(j, 1), :]
        pay[320:321, B : 2 * B] = means[1, pl.ds(j, 1), :]
        for half in range(2):
            pair = jnp.sum(
                jnp.where(lane == 2 * x + half, ids[j].astype(F32), 0.0), axis=1, keepdims=True
            )
            first = jnp.broadcast_to(pair[0:1], (1, B))
            second = jnp.broadcast_to(pair[1:2], (1, B))
            pay[321:322, half * B : (half + 1) * B] = jnp.where(low, first, second)
            pay[322:323, half * B : (half + 1) * B] = jnp.where(low, second, first)
    for copy in copies[3:]:
        copy.wait()


def step_kernel(pay0, pay1, pay2, pay3, local_ref, other_ref, out_ref, pf, rf, inc, vec):
    x, y, z, c = place()
    j = 2 * (x // 2) + c
    same = lax.rem(x, 2) == c
    low = lax.broadcasted_iota(jnp.int32, (64, B), 1) < 64
    for p, pay in enumerate((pay0, pay1, pay2, pay3)):
        source = lax.rem(j - p + 4, 4)
        after = next_block(source, x)
        for row, full in ((0, pf), (B, rf)):
            full[block(source), block(source)] = pay[row : row + B, 0:B]
            beside = pay[row : row + B, B : 2 * B]
            full[block(source), block(after)] = beside
            full[block(after), block(source)] = jnp.transpose(beside)
        for half in range(2):
            r = 2 * source + half
            lanes = slice(half * B, (half + 1) * B)
            tiles = pay[256:320, lanes]
            turned = jnp.concatenate([tiles[:, 64:], tiles[:, :64]], axis=1)
            straight_to = jnp.broadcast_to(pay[321:322, lanes], (64, B))
            turned_to = jnp.broadcast_to(pay[322:323, lanes], (64, B))
            for g in range(4):
                here = jnp.where(low, 2.0 * g, 2.0 * g + 1.0)
                value = jnp.where(
                    straight_to == here, tiles, jnp.where(turned_to == here, turned, 0.0)
                )
                inc[pl.ds(pl.multiple_of(r * 64, 64), 64), g * B : (g + 1) * B] = value
        vec[0:8, block(source)] = jnp.broadcast_to(pay[320:321, 0:B], (8, B))
        vec[8:16, block(source)] = jnp.broadcast_to(pay[320:321, B : 2 * B], (8, B))
    for row, full in ((0, pf), (B, rf)):
        full[block(x), :] = jnp.where(
            same, local_ref[row : row + B, :], other_ref[row : row + B, :]
        )
        for d in (1, 2, 3):
            v = lax.rem(x + d, 4)
            full[block(v), block(x)] = jnp.transpose(full[block(x), block(v)])
    mixed = pf[...] + mm3(split(inc[...]), split(pf[...]))
    mixed = split(mixed)
    precision = split(rf[...])
    lead = split(mm3(split(vec[8:16, :]), precision))
    last = (z == NZ - 1) & (y == NY - 1) & (x == NX - 1) & (c == NC - 1)
    gain = mm3(precision, mixed)
    out_ref[0:W, :] = jnp.where(last, 0.0, gain)
    out_ref[W:FULL, :] = vec[0:8, :] - jnp.where(last, 0.0, mm3(lead, mixed))


def halves(ref, c):
    n = pl.multiple_of(c * HALF, HALF)
    m = pl.multiple_of((1 - c) * HALF, HALF)
    return ref[pl.ds(n, HALF), :], ref[pl.ds(m, HALF), :]


def pair_kernel(own_ref, other_ref, first_ref, second_ref):
    _, _, _, c = place()

    def compose(early, late):
        rows = jnp.concatenate([*halves(early, c), early[W:FULL, :]], axis=0)
        value = mm3(split(rows), split(late[0:W, :]))
        tail = value[W:] + late[W:FULL, :]
        for n, ref in enumerate((first_ref, second_ref)):
            ref[0:HALF, :] = value[n * HALF : (n + 1) * HALF]
            ref[HALF:PAN, :] = tail

    @pl.when(c == 0)
    def _():
        compose(other_ref, own_ref)

    @pl.when(c == 1)
    def _():
        compose(own_ref, other_ref)


def fetch(panels, held, sems, index, c, turned):
    forth, back, far = index + 3 - 2 * c, index + 1 + 2 * c, index + 2
    homes = ((index, c), (index, 1 - c), (forth, c), (forth, 1 - c), (back, 1 - c), (back, c), (far, c), (far, 1 - c))
    for ref, (source, half) in zip(panels, homes):
        slot = lax.rem(source, 4)
        if turned:
            slot = 2 * lax.rem(slot, 2) + slot // 2
        copy = pltpu.make_async_copy(ref, held.at[slot, half], sems.at[slot, half])
        copy.start()


def arrive(panels, held, sems, t):
    for half in range(2):
        pltpu.make_async_copy(panels[0], held.at[t, half], sems.at[t, half]).wait()


def lead_kernel(*refs):
    panels, held, lead_ref, sems = refs[:8], refs[8], refs[9], refs[10]
    _, y, _, c = place()
    fetch(panels, held, sems, y, c, False)
    arrive(panels, held, sems, 3)
    row8 = held[3, 0, HALF:PAN, :]
    for t in (2, 1, 0):
        arrive(panels, held, sems, t)
        row8 = (
            rows_times(row8[:, 0:HALF], held[t, 0, 0:HALF, :])
            + rows_times(row8[:, HALF:W], held[t, 1, 0:HALF, :])
            + held[t, 0, HALF:PAN, :]
        )
    lead_ref[...] = row8


def chain_kernel(along, whole, *refs):
    if whole:
        held, prefix, outs = refs[0], refs[1], refs[2:]
    else:
        panels, held, prefix, outs, sems = refs[:8], refs[8], refs[9], refs[10:-1], refs[-1]
    x, y, _, c = place()
    if not whole:
        fetch(panels, held, sems, x, c, True)
        arrive(panels, held, sems, 3)
    tail = held[3, 0, HALF:PAN, :]
    begin = 0 if whole else c
    rows = jnp.concatenate([held[3, begin, 0:HALF, :], held[3, 1 - begin, 0:HALF, :], tail], axis=0)

    if whole:
        prefix[2] = rows
    for t in (2, 1, 0):
        if not whole:
            arrive(panels, held, sems, t)
        left = split(rows)
        top = split(held[t, 0, 0:HALF, :])
        bottom = split(held[t, 1, 0:HALF, :])
        value = mm3((left[0][:, :HALF], left[1][:, :HALF]), top) + mm3(
            (left[0][:, HALF:], left[1][:, HALF:]), bottom
        )
        rows = jnp.concatenate([value[0:W], value[W:] + held[t, 0, HALF:PAN, :]], axis=0)
        if whole and t > 0:
            prefix[t - 1] = rows
        if not whole and t == 2:
            prefix[pl.ds(pl.multiple_of(c * HALF, HALF), HALF), :] = rows[0:HALF]
            prefix[pl.ds(pl.multiple_of((1 - c) * HALF, HALF), HALF), :] = rows[HALF:W]
            prefix[W:FULL, :] = rows[W:FULL]
    if whole:
        outs[0][...] = rows
    else:
        for n in range(2):
            outs[n][0:HALF, :] = rows[n * HALF : (n + 1) * HALF]
            outs[n][HALF:PAN, :] = rows[W:FULL]


def plane_kernel(map_ref, carried_ref, came_ref, carried_out, out_ref):
    carried = carried_ref[...] + came_ref[...]
    carried_out[...] = carried
    out_ref[...] = rows_times(carried, map_ref[0:W, :]) + map_ref[W:FULL, :]


def columns_kernel(own_ref, other_ref, after_ref, send0, send1):
    x, _, _, c = place()

    def cut(odd):
        for r, send in enumerate((send0, send1)):
            send[...] = odd[:, block(2 * c + lax.rem(x // 2 + r, 2))]

    @pl.when(c == 0)
    def _():
        cut(other_ref)

    @pl.when(c == 1)
    def _():
        cut(own_ref)


def down_kernel(carried_ref, came_ref, cut0_ref, cut1_ref, rows_ref, pairs_ref, held_x, out_ref):
    x, y, _, c = place()

    def apply(row8, ref):
        return rows_times(row8, ref[0:W, :]) + ref[W:FULL, :]

    def pair(row8, t, lanes):
        matrix = jnp.concatenate([held_x[t, 0, 0:HALF, lanes], held_x[t, 1, 0:HALF, lanes]], axis=0)
        return rows_times(row8, matrix) + held_x[t, 0, HALF:PAN, lanes]

    def odd(row8, parity):
        cut = jnp.where(lax.rem(x, 2) == parity, cut0_ref[...], cut1_ref[...])
        return (rows_times(row8, cut[0:W]) + cut[W:FULL])[0:1]

    late = carried_ref[...] + came_ref[...]
    late = jnp.where(y == 3, late, apply(late, rows_ref.at[jnp.minimum(y, 2)]))
    late = jnp.where(c == 1, late, apply(late, pairs_ref))
    early = pair(late, 2 * c + 1, slice(None))
    out_ref[3:4, :] = odd(late, 1)
    out_ref[2:3, :] = pair(late, 2 * c + 1, block(x))[0:1]
    out_ref[1:2, :] = odd(early, 0)
    out_ref[0:1, :] = pair(early, 2 * c, block(x))[0:1]


def shape(*dims):
    return jax.ShapeDtypeStruct(dims, F32)


PARAMS = pltpu.CompilerParams(vmem_limit_bytes=VMEM_LIMIT)
IN_VMEM = pl.BlockSpec(memory_space=pltpu.VMEM)
IN_HBM = pl.BlockSpec(memory_space=pltpu.HBM)
ANYWHERE = pl.BlockSpec(memory_space=pl.ANY)


def gather_panels(first, second, ring, beside=None):
    one, two = move(first, ring), move(second, ring)
    far = move(one, ring)
    if beside is not None:
        two, *beside = lax.optimization_barrier((two, *beside))
    panels = first, second, one, two, move(one, SWAP), move(two, SWAP), far, move(far, SWAP)
    return panels, beside


def lead(panels):
    return pl.pallas_call(
        lead_kernel,
        out_shape=[shape(4, 2, PAN, W), shape(8, W)],
        in_specs=[ANYWHERE] * 8,
        out_specs=[IN_VMEM] * 2,
        scratch_shapes=[pltpu.SemaphoreType.DMA((4, 2))],
        compiler_params=PARAMS,
        name="lead",
    )(*panels)


def chain(along, whole, operands):
    def kernel(*refs):
        chain_kernel(along, whole, *refs)

    outs = [shape(4, 2, PAN, W), shape(FULL, W)] + [shape(PAN, W)] * 2
    if whole:
        outs = [shape(3, FULL, W), shape(FULL, W)]
    return pl.pallas_call(
        kernel,
        out_shape=outs,
        in_specs=[IN_VMEM] if whole else [ANYWHERE] * 8,
        out_specs=[IN_VMEM] * len(outs),
        scratch_shapes=[] if whole else [pltpu.SemaphoreType.DMA((4, 2))],
        compiler_params=PARAMS,
        name="chain_" + along,
    )(*operands)


def in_hbm(value):
    return pltpu.with_memory_space_constraint(value, pltpu.HBM)


def on_device(spread, inverse, tiles, ids, mean, prior):
    *pays, local, other = pl.pallas_call(
        pack_kernel,
        out_shape=[shape(328, HALF)] * 4 + [shape(2 * B, W)] * 2,
        in_specs=[IN_HBM] * 6,
        out_specs=[IN_VMEM] * 6,
        scratch_shapes=[
            pltpu.VMEM((2, 4, B), F32),
            pltpu.VMEM((4, 2, 8), jnp.int32),
            pltpu.SemaphoreType.DMA((31,)),
        ],
        compiler_params=PARAMS,
        name="pack",
    )(*(in_hbm(a) for a in (spread, inverse, tiles, mean, prior, jnp.swapaxes(ids, 1, 2))))
    got = [move(pay, SPREAD[p]) for p, pay in enumerate(pays)]
    other = move(other, SWAP)
    step = pl.pallas_call(
        step_kernel,
        out_shape=shape(FULL, W),
        in_specs=[IN_VMEM] * 6,
        out_specs=IN_VMEM,
        scratch_shapes=[pltpu.VMEM((W, W), F32)] * 3 + [pltpu.VMEM((16, W), F32)],
        compiler_params=PARAMS,
        name="step",
    )(*got, local, other)
    twin = move(step, SWAP)
    pair = pl.pallas_call(
        pair_kernel,
        out_shape=[shape(PAN, W)] * 2,
        in_specs=[IN_VMEM] * 2,
        out_specs=[IN_VMEM] * 2,
        compiler_params=PARAMS,
        name="pair",
    )(step, twin)
    held_x, pairs_map, *row_map = chain("x", False, gather_panels(*pair, RING_X)[0])
    cuts = pl.pallas_call(
        columns_kernel,
        out_shape=[shape(FULL, B)] * 2,
        in_specs=[IN_VMEM] * 2 + [ANYWHERE],
        out_specs=[IN_VMEM] * 2,
        compiler_params=PARAMS,
        name="columns",
    )(step, twin, row_map[0])
    cuts = [move(cut, COLLECT[r]) for r, cut in enumerate(cuts)]
    panels_y, cuts = gather_panels(*row_map, RING_Y, cuts)
    held_y, out = lead(panels_y)
    rows_map, plane_map = chain("y", True, [held_y])
    carried = jnp.zeros((8, W), F32)
    came = jnp.zeros((8, W), F32)
    for i in range(NZ - 1):
        if i > 0:
            carried, out = pl.pallas_call(
                plane_kernel,
                out_shape=[shape(8, W)] * 2,
                in_specs=[IN_VMEM] * 3,
                out_specs=[IN_VMEM] * 2,
                compiler_params=PARAMS,
                name="plane",
            )(plane_map, carried, came)
        came = lax.ppermute(out, "tm", [(t, t - 8) for t in range(64) if t // 8 == 7 - i and t % 2])
    carried = carried + came
    came = lax.ppermute(carried, "tm", [(t, t - 1) for t in range(64) if t % 2])
    return pl.pallas_call(
        down_kernel,
        out_shape=shape(4, B),
        in_specs=[IN_VMEM] * 7,
        out_specs=IN_VMEM,
        compiler_params=PARAMS,
        name="down",
    )(carried, came, *cuts, rows_map, pairs_map, held_x)


def solution(mesh):
    return jax.shard_map(
        on_device,
        mesh=mesh,
        in_specs=(
            P("tm", "state", None),
            P("tm", "state", None),
            P("tm", "state", None, None),
            P("tm", None, None),
            P("tm", "state"),
            P("tm", "state"),
        ),
        out_specs=P("tm", "state"),
        check_vma=False,
    )
```
